32 devices in a mesh: los: 2 (over x), sky: 16 (over z, y, core).
Axes of the slice: x: 2, y: 2, z: 4, core: 2. Of those that a mesh axis runs over, the one named last changes fastest.
Arguments:
- density: bfloat16 [16, 2048, 2048], P('los', 'sky'), may hold values from 0.1 to 10
- refine: int32 [2, 256, 256], P('los', 'sky'), may hold values from 0 to 1, as said below
- weight_low: float32 [16], P('los'), may hold values from 0.1 to 0.5
- weight_high: float32 [16], P('los'), may hold values from 0.6 to 3
Outputs:
- deflection_x: float32 [2048, 2048], P('sky', 'los')
- deflection_y: float32 [2048, 2048], P('sky', 'los')
The draws below stay inside these ranges and needn't reach their ends.
Inputs may be any that keep to these rules, and one draw needn't show every extreme that they name: `refine`: the blocks of one slab and one sky column (one index of los and of sky) hold at most 1024 refined blocks, and in every draw some slab and column holds exactly 1024.
All inputs are finite; a program needn't handle non-finite values.
Results may differ from the reference program's by a relative error of at most 0.0003.
Values may be sent and summed in bfloat16 or wider, within the bound.
A program may use at most 128 MiB of HBM per device.

```python
import math
import jax
import jax.numpy as jnp
from jax import lax

PLANE = 2048
DZ = 8
NZ = 16
CX = 128
REFINED = 1024


def draw_refine(key, part):
    slab_count = NZ // DZ
    column_count = PLANE // CX
    per_device = DZ // 8 * (CX // 8) * (PLANE // 8)
    devices = slab_count * column_count
    keys = jax.random.split(jax.random.fold_in(key, 101), devices)
    ranks = jax.vmap(lambda single: jax.random.permutation(single, per_device))(keys)
    halvings = jax.random.randint(jax.random.fold_in(key, 102), (devices,), 0, 4)
    counts = jnp.right_shift(jnp.full((devices,), REFINED, jnp.int32), halvings)
    busiest = jax.random.randint(jax.random.fold_in(key, 103), (), 0, devices)
    counts = jnp.where(jnp.arange(devices) == busiest, REFINED, counts)
    flags = (ranks < counts[:, None]).astype(jnp.int32)
    flags = flags.reshape(slab_count, column_count, DZ // 8, CX // 8, PLANE // 8)
    return flags.transpose(0, 2, 1, 3, 4).reshape(NZ // 8, PLANE // 8, PLANE // 8)


def draw_density(key, part):
    rough_span = 1.4
    ramp_span = 0.7
    noise_span = 0.15
    step_low = 0.15
    step_high = 0.35
    rough = jax.random.uniform(jax.random.fold_in(key, 211), (PLANE, PLANE), jnp.float32, -rough_span, rough_span)
    increments = jax.random.uniform(jax.random.fold_in(key, 212), (NZ,), jnp.float32, step_low, step_high)
    offset = jax.random.uniform(jax.random.fold_in(key, 213), (), jnp.float32)
    phase = offset + jnp.cumsum(increments)
    ramp = ramp_span * (2.0 * (phase - jnp.floor(phase)) - 1.0)
    noise = jax.random.uniform(jax.random.fold_in(key, 214), (NZ, PLANE, PLANE), jnp.float32, -noise_span, noise_span)
    logs = rough[None, :, :] + ramp[:, None, None] + noise
    return jnp.exp(logs).astype(jnp.bfloat16)


def block_levels(key, dims, cuts, smallest, top_value):
    loudness, own = 1.0, jax.random.fold_in(key, 6)
    for dim, parts in cuts:
        draws = jnp.exp(jax.random.uniform(jax.random.fold_in(own, dim), (parts,), jnp.float32, smallest / len(cuts), top_value / len(cuts)))
        loudness = loudness * jnp.repeat(draws, dims[dim] // parts).reshape([-1 if axis == dim else 1 for axis in range(len(dims))])
    return loudness


def setup_inputs(seed: int = 0) -> dict:
    splits = jax.random.split(jax.random.key(seed), 5)
    density = draw_density(jax.random.fold_in(splits[4], 71), 0)
    refine = draw_refine(jax.random.fold_in(splits[4], 71), 0)
    weight_low = jnp.clip(jnp.exp(math.log(0.5) - 1.609438 * jax.random.uniform(splits[2], (NZ,), jnp.float32) ** block_levels(splits[2], (NZ,), ((0, 2),), -0.2, 0.2)), 0.1, 0.5)
    weight_high = jnp.clip(jnp.exp(math.log(3.0) - 1.60943787 * jax.random.uniform(splits[3], (NZ,), jnp.float32) ** block_levels(splits[3], (NZ,), ((0, 2),), -0.2, 0.2)), 0.6, 3.0)
    return dict(density=density, refine=refine, weight_low=weight_low, weight_high=weight_high)


def minmod(former, latter):
    return 0.5 * (jnp.sign(former) + jnp.sign(latter)) * jnp.minimum(jnp.abs(former), jnp.abs(latter))


def spread(field, dimension):
    return 0.75 * field + 0.125 * (jnp.roll(field, 1, dimension) + jnp.roll(field, -1, dimension))


def slanted(field, dimension):
    return (jnp.roll(field, 1, dimension) - jnp.roll(field, -1, dimension)) / 32.0


def reference(density, refine, weight_low, weight_high):
    layers = density.shape[0]
    plane = density.shape[1]

    def layer(totals, position):
        below = lax.dynamic_index_in_dim(density, jnp.maximum(position - 1, 0), 0, keepdims=False).astype(jnp.float32)
        centre = lax.dynamic_index_in_dim(density, position, 0, keepdims=False).astype(jnp.float32)
        above = lax.dynamic_index_in_dim(density, jnp.minimum(position + 1, layers - 1), 0, keepdims=False).astype(jnp.float32)
        grad_z = minmod(above - centre, centre - below)
        grad_x = minmod(jnp.roll(centre, -1, 0) - centre, centre - jnp.roll(centre, 1, 0))
        grad_y = minmod(jnp.roll(centre, -1, 1) - centre, centre - jnp.roll(centre, 1, 1))
        coarse = lax.dynamic_index_in_dim(refine, position // 8, 0, keepdims=False).astype(jnp.float32)
        marked = jnp.repeat(jnp.repeat(coarse, 8, 0), 8, 1)
        low = lax.dynamic_index_in_dim(weight_low, position, 0, keepdims=False)
        high = lax.dynamic_index_in_dim(weight_high, position, 0, keepdims=False)
        average = 0.5 * (low + high)
        weighted = average * centre
        base, refined_base, tilt_z, tilt_x, tilt_y = totals
        return (base + weighted,
                refined_base + marked * weighted,
                tilt_z + marked * (0.125 * (high - low)) * grad_z,
                tilt_x + marked * average * grad_x,
                tilt_y + marked * average * grad_y), None

    blank = jnp.zeros((plane, plane), jnp.float32)
    totals, leftover = lax.scan(layer, (blank, blank, blank, blank, blank), jnp.arange(layers, dtype=jnp.int32))
    base, refined_base, tilt_z, tilt_x, tilt_y = totals
    smoothed = spread(refined_base + tilt_z, 1) + slanted(tilt_y, 1)
    kappa = (base - refined_base + spread(smoothed, 0) + slanted(spread(tilt_x, 1), 0)) / jnp.float32(layers)
    spectrum = jnp.fft.fft2(kappa)
    wave = 2.0 * jnp.pi * jnp.fft.fftfreq(plane)
    wave_x = wave[:, None]
    wave_y = wave[None, :]
    squared = wave_x * wave_x + wave_y * wave_y
    at_anchor = squared == 0
    potential = jnp.where(at_anchor, 0.0, -2.0 / jnp.where(at_anchor, 1.0, squared)) * spectrum
    deflection_x = jnp.real(jnp.fft.ifft2(1j * wave_x * potential)).astype(jnp.float32)
    deflection_y = jnp.real(jnp.fft.ifft2(1j * wave_y * potential)).astype(jnp.float32)
    return (deflection_x, deflection_y)
```

```python
import functools
import math

import jax
import jax.numpy as jnp
import numpy as np
from jax import lax
from jax.experimental import pallas as pl
from jax.experimental.pallas import tpu as pltpu
from jax.sharding import PartitionSpec as P

LANES = 128
SUB = 8
VMEM = pl.BlockSpec(memory_space=pltpu.VMEM)
SMEM = pl.BlockSpec(memory_space=pltpu.SMEM)


def median0(a, b):
    return jnp.maximum(jnp.minimum(a, b), jnp.minimum(jnp.maximum(a, b), 0.0))


def add(p, q):
    im = q[1] if p[1] is None else (p[1] if q[1] is None else p[1] + q[1])
    return (p[0] + q[0], im)


def sub(p, q):
    if q[1] is None:
        return (p[0] - q[0], p[1])
    return (p[0] - q[0], -q[1] if p[1] is None else p[1] - q[1])


def turn(p, angle):
    c, s = math.cos(angle), math.sin(angle)
    re, im = p
    if abs(s) < 1e-12:
        return p if c > 0 else (-re, None if im is None else -im)
    if abs(c) < 1e-12:
        sign = 1.0 if s > 0 else -1.0
        if im is None:
            return (jnp.zeros_like(re), sign * re)
        return (-im, re) if s > 0 else (im, -re)
    if im is None:
        return (c * re, s * re)
    return (c * re - s * im, s * re + c * im)


def fft_list(items, flip):
    count = len(items)
    if count == 1:
        return items
    even = fft_list(items[0::2], flip)
    odd = fft_list(items[1::2], flip)
    first, second = [], []
    for k in range(count // 2):
        w = turn(odd[k], flip * 2.0 * math.pi * k / count)
        first.append(add(even[k], w))
        second.append(sub(even[k], w))
    return first + second


def row_table(width):
    tiles = width // LANES
    classes = tiles // 2
    half = LANES // 2
    t = np.arange(LANES)
    table = np.zeros((classes, 2 * LANES, 2 * LANES))

    def angles(n):
        return 2.0 * np.pi * ((n[:, None] * t[None, :]) % width) / width

    for c in range(classes):
        if c == 0:
            j = np.arange(half)
            low = angles(tiles * j)
            high = angles(tiles * j + classes)
            table[0, :half, :LANES] = np.cos(low)
            table[0, half:LANES, LANES:] = np.cos(high)
            table[0, LANES : LANES + half, :LANES] = -np.sin(low)
            table[0, LANES, :LANES] = np.cos(np.pi * t)
            table[0, LANES + half :, LANES:] = -np.sin(high)
        else:
            a = angles(c + tiles * np.arange(LANES))
            table[c, :LANES, :LANES] = np.cos(a)
            table[c, :LANES, LANES:] = np.sin(a)
            table[c, LANES:, :LANES] = -np.sin(a)
            table[c, LANES:, LANES:] = np.cos(a)
    return jnp.asarray(table, jnp.float32)


def tile_table(width):
    tiles = width // LANES
    classes = tiles // 2
    s = np.arange(tiles)
    table = np.zeros((classes, 2 * tiles))
    for c in range(classes):
        if c == 0:
            table[c, 0::2] = 1.0
            table[c, 1::2] = np.where(s % 2 == 0, 1.0, -1.0)
        else:
            table[c, 0::2] = np.cos(2.0 * np.pi * s * c / tiles)
            table[c, 1::2] = -np.sin(2.0 * np.pi * s * c / tiles)
    return jnp.asarray(table, jnp.float32)


def column_tables(length, sky):
    rows = length // sky
    t = np.arange(rows)
    a = 2.0 * np.pi * (t[:, None] * t[None, :] % rows) / rows
    c, s = np.cos(a), np.sin(a)
    forward = np.block([[c, -s], [s, c]])
    b = 2.0 * np.pi * (np.arange(sky)[:, None] * t[None, :]) / length
    twist = np.stack([np.cos(b), np.sin(b)], axis=1)
    return jnp.asarray(forward, jnp.float32), jnp.asarray(twist, jnp.float32)


def dot(a, b, dims):
    return lax.dot_general(
        a, b, (dims, ((), ())), precision=lax.Precision.HIGHEST, preferred_element_type=jnp.float32
    )


def layer_kernel(
    density, below, above, before, after, refine, average, slope, keep, out, cells, base_s, smooth_s, tilt_s
):
    layers, rows, width = density.shape
    tiles = width // LANES
    blocks = refine.shape[0]
    coarse = refine.shape[1]
    deep = 16
    for z in range(layers):
        rims = [before[z : z + 1, :].astype(jnp.float32), after[z : z + 1, :].astype(jnp.float32)]
        cells[z + 1, SUB - 1 : SUB, :] = rims[0]
        cells[z + 1, SUB + rows : SUB + rows + 1, :] = rims[1]

    def fill(r, carry):
        start = pl.multiple_of(r * deep, deep)
        into = pl.ds(pl.multiple_of(start + SUB, SUB), deep)
        cells[0, into, :] = below[pl.ds(start, deep), :].astype(jnp.float32)
        cells[layers + 1, into, :] = above[pl.ds(start, deep), :].astype(jnp.float32)
        for z in range(layers):
            cells[z + 1, into, :] = density[z, pl.ds(start, deep), :].astype(jnp.float32)
        return carry

    lax.fori_loop(0, rows // deep, fill, 0)
    blank = jnp.zeros((2 * SUB, width), jnp.float32)
    for ref in (smooth_s, tilt_s):
        ref[0 : 2 * SUB, :] = blank
        ref[rows + 2 * SUB : rows + 4 * SUB, :] = blank
    base_s[0:SUB, :] = blank[:SUB]
    base_s[rows + SUB : rows + 2 * SUB, :] = blank[:SUB]
    column = lax.broadcasted_iota(jnp.int32, (coarse, width), 1)
    line = lax.broadcasted_iota(jnp.int32, (coarse, width), 0)
    wide = width // coarse
    inside = (column >= line * wide) & (column < line * wide + wide)
    stretch = jnp.where(inside, 1.0, 0.0).astype(jnp.bfloat16)
    marks = jnp.dot(
        refine[...].astype(jnp.float32).astype(jnp.bfloat16), stretch, preferred_element_type=jnp.float32
    )
    for r in range(blocks):
        base_s[SUB * (r + 1) : SUB * (r + 2), :] = jnp.broadcast_to(marks[r : r + 1], (SUB, width))

    def spread(field):
        return 0.75 * field + 0.125 * (pltpu.roll(field, 1, 1) + pltpu.roll(field, width - 1, 1))

    def chunk(r, carry):
        start = pl.multiple_of(r * SUB, SUB)
        here = pl.ds(pl.multiple_of(start + SUB, SUB), SUB)
        mid = cells[1, here, :]
        step_z = keep[0] * (mid - cells[0, here, :])
        base = jnp.zeros((SUB, width), jnp.float32)
        tilt_z, tilt_x, tilt_y = base, base, base
        for z in range(layers):
            above_mid = cells[z + 2, here, :]
            next_z = above_mid - mid
            if z == layers - 1:
                next_z = keep[1] * next_z
            w = cells[z + 1, pl.ds(start, 3 * SUB), :]
            up, down = w[SUB - 1 : 2 * SUB - 1], w[SUB + 1 : 2 * SUB + 1]
            step_y = pltpu.roll(mid, width - 1, 1) - mid
            back_y = pltpu.roll(step_y, 1, 1)
            base = base + average[z] * mid
            tilt_z = tilt_z + slope[z] * median0(next_z, step_z)
            tilt_x = tilt_x + average[z] * median0(down - mid, mid - up)
            tilt_y = tilt_y + average[z] * median0(step_y, back_y)
            mid, step_z = above_mid, next_z
        mark = base_s[here, :]
        refined = mark * base
        base_s[here, :] = base - refined
        tilt_y = mark * tilt_y
        into = pl.ds(pl.multiple_of(start + 2 * SUB, SUB), SUB)
        smooth_s[into, :] = spread(refined + mark * tilt_z) + (
            pltpu.roll(tilt_y, 1, 1) - pltpu.roll(tilt_y, width - 1, 1)
        ) * (1.0 / 32.0)
        tilt_s[into, :] = spread(mark * tilt_x)
        return carry

    lax.fori_loop(0, rows // SUB, chunk, 0)

    def finish(r, carry):
        start = pl.multiple_of(r * SUB, SUB)
        a = smooth_s[pl.ds(start, 3 * SUB), :]
        b = tilt_s[pl.ds(start, 3 * SUB), :]
        prior, mid, later = slice(SUB - 1, 2 * SUB - 1), slice(SUB, 2 * SUB), slice(SUB + 1, 2 * SUB + 1)
        deposit = (
            base_s[pl.ds(start, SUB), :]
            + 0.75 * a[mid]
            + 0.125 * (a[prior] + a[later])
            + (b[prior] - b[later]) * (1.0 / 32.0)
        )
        parts = [(deposit[:, LANES * s : LANES * (s + 1)], None) for s in range(tiles)]
        modes = fft_list(parts, -1.0)
        for c in range(tiles // 2):
            pair = (modes[0][0], modes[tiles // 2][0]) if c == 0 else modes[c]
            for j in range(2):
                out[c, j, pl.ds(start, SUB), :] = pair[j]
        return carry

    lax.fori_loop(0, rows // SUB + 2, finish, 0)


def row_kernel(place, tiles, table, out):
    sources, groups, pair, padded, lanes = tiles.shape
    rows = padded - 2 * SUB
    sky, part = out.shape[0], out.shape[3]
    line = lax.broadcasted_iota(jnp.int32, (rows, lanes), 0)
    for g in range(groups):
        sides = []
        for j in range(pair):
            total = tiles[0, g, j]
            for source in range(1, sources):
                total = total + tiles[source, g, j]
            side = total[SUB : SUB + rows]
            side = side + jnp.where(line == 0, total[0:1], 0.0)
            side = side + jnp.where(line == rows - 1, total[padded - 1 : padded], 0.0)
            sides.append(side)
        modes = dot(table[place[0] * groups + g], jnp.concatenate(sides, axis=1), ((1,), (1,)))
        for d in range(sky):
            for j in range(pair):
                begin = j * lanes + d * part
                out[d, g, j] = modes[begin : begin + part]


def column_kernel(length, layers, place, modes, forward, twist, out):
    sky, groups, pair, part, rows = modes.shape
    classes = length // LANES // 2
    tiles = 2 * classes
    count = groups * part
    extra = SUB
    total = count + extra
    line = lax.broadcasted_iota(jnp.int32, (total, rows), 0)
    lane = lax.broadcasted_iota(jnp.int32, (total, rows), 1)
    first = (place[0] == 0) & (place[1] == 0)
    packed = (line == 0) & first
    group = line // part
    kind = place[0] * groups + group
    j = place[1] * part + line % part
    half = LANES // 2
    n = jnp.where(kind == 0, jnp.where(j < half, tiles * j, tiles * (j - half) + classes), kind + tiles * j)
    n = jnp.where(n >= length // 2, n - length, n)
    n = jnp.where(line >= count, length // 2, n)
    ny = n.astype(jnp.float32)
    odd_y = jnp.where(n == length // 2, 0.0, ny)
    single = packed | (line >= count)
    unit = 2.0 * math.pi / length
    weight = jnp.where(single, 1.0, 2.0) * (-2.0 / (unit * float(length) * float(length) * float(layers)))
    zero = jnp.zeros((extra, rows), jnp.float32)
    items = []
    for s in range(sky):
        re = jnp.concatenate([modes[s, g, 0] for g in range(groups)], axis=0)
        im = jnp.concatenate([modes[s, g, 1] for g in range(groups)], axis=0)
        spare = jnp.broadcast_to(im[0:1], (extra, rows))
        re = jnp.concatenate([re, spare], axis=0)
        im = jnp.concatenate([im, zero], axis=0)
        items.append((re, jnp.where(packed, 0.0, im)))
    items = fft_list(items, -1.0)
    turned = []
    for k, (re, im) in enumerate(items):
        c, s = twist[k, 0:1, :], twist[k, 1:2, :]
        turned.append(jnp.concatenate([re * c + im * s, im * c - re * s], axis=1))
    spectrum = dot(jnp.concatenate(turned, axis=0), forward[...], ((1,), (0,)))
    fields = ([], [])
    for k in range(sky):
        here = spectrum[k * total : (k + 1) * total]
        re, im = here[:, :rows], here[:, rows:]
        nx = k + sky * lane
        nx = jnp.where(nx >= length // 2, nx - length, nx)
        odd_x = jnp.where(nx == -(length // 2), 0, nx).astype(jnp.float32)
        square = nx.astype(jnp.float32) * nx.astype(jnp.float32) + ny * ny
        factor = jnp.where(square == 0.0, 0.0, weight / jnp.where(square == 0.0, 1.0, square))
        for field, odd in ((0, odd_x), (1, odd_y)):
            scale = odd * factor
            fields[field].append(jnp.concatenate([-scale * im, scale * re], axis=1))
    for field in range(2):
        values = dot(jnp.concatenate(fields[field], axis=0), forward[...], ((1,), (1,)))
        items = []
        for k in range(sky):
            here = values[k * total : (k + 1) * total]
            re, im = here[:, :rows], here[:, rows:]
            c, s = twist[k, 0:1, :], twist[k, 1:2, :]
            items.append((re * c - im * s, im * c + re * s))
        items = fft_list(items, 1.0)
        for s in range(sky):
            re, im = items[s]
            im = jnp.where(packed, jnp.broadcast_to(re[count : count + 1], (total, rows)), im)
            for g in range(groups):
                out[s, field, g, 0] = re[g * part : (g + 1) * part]
                out[s, field, g, 1] = im[g * part : (g + 1) * part]


def plane_kernel(place, modes, table, mix, out):
    sky, fields, groups, pair, part, rows = modes.shape
    parts, width = out.shape[0], out.shape[3]
    tiles = parts * width // LANES
    for field in range(fields):
        pieces = []
        for g in range(groups):
            z = jnp.concatenate([modes[d, field, g, j] for j in range(pair) for d in range(sky)], axis=0)
            both = dot(z, table[place[0] * groups + g], ((0,), (0,)))
            pieces.append((both[:, :LANES], both[:, LANES:]))
        for s in range(tiles):
            total = None
            for g in range(groups):
                kind = place[0] * groups + g
                term = mix[kind, 2 * s] * pieces[g][0] + mix[kind, 2 * s + 1] * pieces[g][1]
                total = term if total is None else total + term
            at = s * LANES
            out[at // width, field, :, at % width : at % width + LANES] = total


def call(kernel, shape, specs, scratch=()):
    return pl.pallas_call(
        kernel,
        out_shape=jax.ShapeDtypeStruct(shape, jnp.float32),
        in_specs=specs,
        out_specs=VMEM,
        scratch_shapes=list(scratch),
        compiler_params=pltpu.CompilerParams(vmem_limit_bytes=60 * 1024 * 1024),
    )


def body(density, refine, weight_low, weight_high):
    los_count = lax.axis_size("los")
    sky_count = lax.axis_size("sky")
    los = lax.axis_index("los")
    sky = lax.axis_index("sky")
    layers, rows, width = density.shape
    length = rows * sky_count
    tiles = width // LANES
    classes = tiles // 2
    groups = classes // los_count
    part = LANES // sky_count
    place = jnp.stack([los, sky]).astype(jnp.int32)
    onward = [(i, i + 1) for i in range(los_count - 1)]
    back = [(i + 1, i) for i in range(los_count - 1)]
    ring = [(i, (i + 1) % sky_count) for i in range(sky_count)]
    gnir = [((i + 1) % sky_count, i) for i in range(sky_count)]
    below = lax.ppermute(density[layers - 1], "los", onward)
    above = lax.ppermute(density[0], "los", back)
    before = lax.ppermute(density[:, rows - 1, :], "sky", ring)
    after = lax.ppermute(density[:, 0, :], "sky", gnir)
    average = 0.5 * (weight_low + weight_high)
    slope = 0.125 * (weight_high - weight_low)
    keep = jnp.stack([los > 0, los < los_count - 1]).astype(jnp.float32)
    padded = rows + 2 * SUB
    folded = call(
        layer_kernel,
        (classes, 2, padded, LANES),
        [VMEM] * 6 + [SMEM] * 3,
        [
            pltpu.VMEM((layers + 2, padded, width), jnp.float32),
            pltpu.VMEM((padded, width), jnp.float32),
            pltpu.VMEM((rows + 4 * SUB, width), jnp.float32),
            pltpu.VMEM((rows + 4 * SUB, width), jnp.float32),
        ],
    )(density, below, above, before, after, refine[0], average, slope, keep)
    to_before = folded[:, :, SUB - 1 : SUB]
    to_after = folded[:, :, rows + SUB : rows + SUB + 1]
    from_before = lax.ppermute(to_after, "sky", ring)
    from_after = lax.ppermute(to_before, "sky", gnir)
    folded = lax.dynamic_update_slice(folded, from_before, (0, 0, 0, 0))
    folded = lax.dynamic_update_slice(folded, from_after, (0, 0, padded - 1, 0))
    folded = folded.reshape(los_count, groups, 2, padded, LANES)
    folded = lax.all_to_all(folded, "los", split_axis=0, concat_axis=0, tiled=True)
    table = row_table(width)
    modes = call(row_kernel, (sky_count, groups, 2, part, rows), [SMEM, VMEM, VMEM])(place, folded, table)
    modes = lax.all_to_all(modes, "sky", split_axis=0, concat_axis=0, tiled=True)
    forward, twist = column_tables(length, sky_count)
    fields = call(
        functools.partial(column_kernel, length, layers * los_count),
        (sky_count, 2, groups, 2, part, rows),
        [SMEM, VMEM, VMEM, VMEM],
    )(place, modes, forward, twist)
    fields = lax.all_to_all(fields, "sky", split_axis=0, concat_axis=0, tiled=True)
    plane = call(plane_kernel, (los_count, 2, rows, width // los_count), [SMEM, VMEM, VMEM, SMEM])(
        place, fields, table, tile_table(width)
    )
    plane = lax.all_to_all(plane, "los", split_axis=0, concat_axis=0, tiled=True)
    plane = jnp.sum(plane, axis=0)
    return (plane[0], plane[1])


def solution(mesh):
    placed = (P("los", "sky", None), P("los", "sky", None), P("los"), P("los"))
    return jax.shard_map(
        body,
        mesh=mesh,
        in_specs=placed,
        out_specs=(P("sky", "los"), P("sky", "los")),
        check_vma=False,
    )
```

```python
import functools
import math

import jax
import jax.numpy as jnp
import numpy as np
from jax import lax
from jax.experimental import pallas as pl
from jax.experimental.pallas import tpu as pltpu
from jax.sharding import PartitionSpec as P

LANES = 128
SUB = 8
VMEM = pl.BlockSpec(memory_space=pltpu.VMEM)
SMEM = pl.BlockSpec(memory_space=pltpu.SMEM)


def median0(a, b):
    return jnp.maximum(jnp.minimum(a, b), jnp.minimum(jnp.maximum(a, b), 0.0))


def add(p, q):
    im = q[1] if p[1] is None else (p[1] if q[1] is None else p[1] + q[1])
    return (p[0] + q[0], im)


def sub(p, q):
    if q[1] is None:
        return (p[0] - q[0], p[1])
    return (p[0] - q[0], -q[1] if p[1] is None else p[1] - q[1])


def turn(p, angle):
    c, s = math.cos(angle), math.sin(angle)
    re, im = p
    if abs(s) < 1e-12:
        return p if c > 0 else (-re, None if im is None else -im)
    if abs(c) < 1e-12:
        sign = 1.0 if s > 0 else -1.0
        if im is None:
            return (jnp.zeros_like(re), sign * re)
        return (-im, re) if s > 0 else (im, -re)
    if im is None:
        return (c * re, s * re)
    return (c * re - s * im, s * re + c * im)


def fft_list(items, flip):
    count = len(items)
    if count == 1:
        return items
    even = fft_list(items[0::2], flip)
    odd = fft_list(items[1::2], flip)
    first, second = [], []
    for k in range(count // 2):
        w = turn(odd[k], flip * 2.0 * math.pi * k / count)
        first.append(add(even[k], w))
        second.append(sub(even[k], w))
    return first + second


def row_table(width):
    tiles = width // LANES
    classes = tiles // 2
    half = LANES // 2
    t = np.arange(LANES)
    table = np.zeros((classes, 2 * LANES, 2 * LANES))

    def angles(n):
        return 2.0 * np.pi * ((n[:, None] * t[None, :]) % width) / width

    for c in range(classes):
        if c == 0:
            j = np.arange(half)
            low = angles(tiles * j)
            high = angles(tiles * j + classes)
            table[0, :half, :LANES] = np.cos(low)
            table[0, half:LANES, LANES:] = np.cos(high)
            table[0, LANES : LANES + half, :LANES] = -np.sin(low)
            table[0, LANES, :LANES] = np.cos(np.pi * t)
            table[0, LANES + half :, LANES:] = -np.sin(high)
        else:
            a = angles(c + tiles * np.arange(LANES))
            table[c, :LANES, :LANES] = np.cos(a)
            table[c, :LANES, LANES:] = np.sin(a)
            table[c, LANES:, :LANES] = -np.sin(a)
            table[c, LANES:, LANES:] = np.cos(a)
    return jnp.asarray(table, jnp.float32)


def tile_table(width):
    tiles = width // LANES
    classes = tiles // 2
    s = np.arange(tiles)
    table = np.zeros((classes, 2 * tiles))
    for c in range(classes):
        if c == 0:
            table[c, 0::2] = 1.0
            table[c, 1::2] = np.where(s % 2 == 0, 1.0, -1.0)
        else:
            table[c, 0::2] = np.cos(2.0 * np.pi * s * c / tiles)
            table[c, 1::2] = -np.sin(2.0 * np.pi * s * c / tiles)
    return jnp.asarray(table, jnp.float32)


def column_tables(length, sky):
    rows = length // sky
    t = np.arange(rows)
    a = 2.0 * np.pi * (t[:, None] * t[None, :] % rows) / rows
    c, s = np.cos(a), np.sin(a)
    forward = np.block([[c, -s], [s, c]])
    b = 2.0 * np.pi * (np.arange(sky)[:, None] * t[None, :]) / length
    twist = np.stack([np.cos(b), np.sin(b)], axis=1)
    return jnp.asarray(forward, jnp.float32), jnp.asarray(twist, jnp.float32)


def dot(a, b, dims):
    return lax.dot_general(
        a, b, (dims, ((), ())), precision=lax.Precision.HIGHEST, preferred_element_type=jnp.float32
    )


def sums_kernel(density, average, slope, out, cells):
    layers, rows, width = density.shape
    deep = 16
    last = density[:, rows - deep : rows, :]
    head = density[:, 0:deep, :]
    for z in range(layers):
        cells[z, SUB - 1 : SUB, :] = head[z].astype(jnp.float32)[0:1]
        cells[z, SUB + rows : SUB + rows + 1, :] = last[z].astype(jnp.float32)[deep - 1 : deep]

    def fill(r, carry):
        start = pl.multiple_of(r * deep, deep)
        into = pl.ds(pl.multiple_of(start + SUB, SUB), deep)
        for z in range(layers):
            cells[z, into, :] = density[z, pl.ds(start, deep), :].astype(jnp.float32)
        return carry

    lax.fori_loop(0, rows // deep, fill, 0)

    def chunk(r, carry):
        start = pl.multiple_of(r * SUB, SUB)
        here = pl.ds(pl.multiple_of(start + SUB, SUB), SUB)
        mid = cells[0, here, :]
        step_z = None
        base = jnp.zeros((SUB, width), jnp.float32)
        tilt_z, tilt_x, tilt_y = base, base, base
        for z in range(layers):
            w = cells[z, pl.ds(start, 3 * SUB), :]
            up, down = w[SUB - 1 : 2 * SUB - 1], w[SUB + 1 : 2 * SUB + 1]
            step_y = pltpu.roll(mid, width - 1, 1) - mid
            back_y = pltpu.roll(step_y, 1, 1)
            base = base + average[z] * mid
            tilt_x = tilt_x + average[z] * median0(down - mid, mid - up)
            tilt_y = tilt_y + average[z] * median0(step_y, back_y)
            if z < layers - 1:
                above = cells[z + 1, here, :]
                next_z = above - mid
                if z > 0:
                    tilt_z = tilt_z + slope[z] * median0(next_z, step_z)
                mid, step_z = above, next_z
        rows_at = pl.ds(start, SUB)
        out[0, rows_at, :] = base
        out[1, rows_at, :] = tilt_z
        out[2, rows_at, :] = tilt_x
        out[3, rows_at, :] = tilt_y
        return carry

    lax.fori_loop(0, rows // SUB, chunk, 0)


def edge_kernel(
    sums, low, high, below, above, before, first, second, former, final, after, refine, column_average, slope, keep,
    place, out, rims, base_s, smooth_s, tilt_s
):
    rows, width = below.shape
    tiles = width // LANES
    los_count, groups = out.shape[0], out.shape[1]
    blocks, coarse = refine.shape
    deep = 16
    weight = column_average[...]

    def rim_slope(one, two, three):
        one, two, three = [ref[...].astype(jnp.float32) for ref in (one, two, three)]
        return jnp.sum(weight * median0(three - two, two - one), axis=0, keepdims=True)

    fix_first = rim_slope(before, first, second)
    fix_last = rim_slope(former, final, after)
    blank = jnp.zeros((2 * SUB, width), jnp.float32)
    for ref in (smooth_s, tilt_s):
        ref[0 : 2 * SUB, :] = blank
        ref[rows + 2 * SUB : rows + 4 * SUB, :] = blank
    base_s[0:SUB, :] = blank[:SUB]
    base_s[rows + SUB : rows + 2 * SUB, :] = blank[:SUB]
    column = lax.broadcasted_iota(jnp.int32, (coarse, width), 1)
    line = lax.broadcasted_iota(jnp.int32, (coarse, width), 0)
    wide = width // coarse
    inside = (column >= line * wide) & (column < line * wide + wide)
    stretch = jnp.where(inside, 1.0, 0.0).astype(jnp.bfloat16)
    marks = jnp.dot(
        refine[...].astype(jnp.float32).astype(jnp.bfloat16), stretch, preferred_element_type=jnp.float32
    )
    for r in range(blocks):
        base_s[SUB * (r + 1) : SUB * (r + 2), :] = jnp.broadcast_to(marks[r : r + 1], (SUB, width))

    def spread(field):
        return 0.75 * field + 0.125 * (pltpu.roll(field, 1, 1) + pltpu.roll(field, width - 1, 1))

    end = low.shape[0]

    def chunk(r, carry):
        start = pl.multiple_of(r * deep, deep)
        here = pl.ds(start, deep)
        base, tilt_z, tilt_x, tilt_y = [sums[i, here, :] for i in range(4)]
        v0, v1 = [low[i, here, :].astype(jnp.float32) for i in range(2)]
        v6, v7 = [high[i, here, :].astype(jnp.float32) for i in range(2)]
        under, over = below[here, :].astype(jnp.float32), above[here, :].astype(jnp.float32)
        tilt_z = tilt_z + slope[0] * median0(v1 - v0, keep[0] * (v0 - under))
        tilt_z = tilt_z + slope[slope.shape[0] - 1] * median0(keep[1] * (over - v7), v7 - v6)
        at = lax.broadcasted_iota(jnp.int32, (deep, width), 0) + start
        tilt_x = tilt_x + jnp.where(at == 0, fix_first, 0.0) + jnp.where(at == rows - 1, fix_last, 0.0)
        ours = pl.ds(pl.multiple_of(start + SUB, SUB), deep)
        mark = base_s[ours, :]
        refined = mark * base
        base_s[ours, :] = base - refined
        tilt_y = mark * tilt_y
        into = pl.ds(pl.multiple_of(start + 2 * SUB, SUB), deep)
        smooth_s[into, :] = spread(refined + mark * tilt_z) + (
            pltpu.roll(tilt_y, 1, 1) - pltpu.roll(tilt_y, width - 1, 1)
        ) * (1.0 / 32.0)
        tilt_s[into, :] = spread(mark * tilt_x)
        return carry

    lax.fori_loop(0, rows // deep, chunk, 0)

    def pairs(start):
        a = smooth_s[pl.ds(start, 3 * SUB), :]
        b = tilt_s[pl.ds(start, 3 * SUB), :]
        prior, mid, later = slice(SUB - 1, 2 * SUB - 1), slice(SUB, 2 * SUB), slice(SUB + 1, 2 * SUB + 1)
        deposit = (
            base_s[pl.ds(start, SUB), :]
            + 0.75 * a[mid]
            + 0.125 * (a[prior] + a[later])
            + (b[prior] - b[later]) * (1.0 / 32.0)
        )
        parts = [(deposit[:, LANES * s : LANES * (s + 1)], None) for s in range(tiles)]
        modes = fft_list(parts, -1.0)
        return [(modes[0][0], modes[tiles // 2][0])] + modes[1 : tiles // 2]

    def finish(r, carry):
        into = pl.ds(pl.multiple_of(r * SUB, SUB), SUB)
        for c, pair in enumerate(pairs(pl.multiple_of((r + 1) * SUB, SUB))):
            relative = lax.rem(c // groups - place[0] + los_count, los_count)
            for j in range(2):
                out[relative, c % groups, j, into, :] = pair[j]
        return carry

    lax.fori_loop(0, rows // SUB, finish, 0)
    for edge, (start, row) in enumerate(((0, SUB - 1), (rows + SUB, 0))):
        for c, pair in enumerate(pairs(start)):
            for j in range(2):
                rims[edge, c, j : j + 1, :] = pair[j][row : row + 1]


def row_kernel(place, own, *refs):
    *others, rims, table, out = refs
    groups, pair, rows, lanes = own.shape
    sky, part = out.shape[0], out.shape[3]
    line = lax.broadcasted_iota(jnp.int32, (rows, lanes), 0)
    for g in range(groups):
        sides = []
        for j in range(pair):
            side = own[g, j]
            for other in others:
                side = side + other[g, j]
            side = side + jnp.where(line == 0, rims[0, g, j : j + 1, :], 0.0)
            side = side + jnp.where(line == rows - 1, rims[1, g, j : j + 1, :], 0.0)
            sides.append(side)
        modes = dot(table[place[0] * groups + g], jnp.concatenate(sides, axis=1), ((1,), (1,)))
        for d in range(sky):
            for j in range(pair):
                begin = j * lanes + d * part
                out[d, g, j] = modes[begin : begin + part]


def column_kernel(length, layers, place, modes, forward, twist, *outs):
    sky, groups, pair, part, rows = modes.shape
    classes = length // LANES // 2
    tiles = 2 * classes
    count = groups * part
    extra = SUB
    total = count + extra
    line = lax.broadcasted_iota(jnp.int32, (total, rows), 0)
    lane = lax.broadcasted_iota(jnp.int32, (total, rows), 1)
    first = (place[0] == 0) & (place[1] == 0)
    packed = (line == 0) & first
    group = line // part
    kind = place[0] * groups + group
    j = place[1] * part + line % part
    half = LANES // 2
    n = jnp.where(kind == 0, jnp.where(j < half, tiles * j, tiles * (j - half) + classes), kind + tiles * j)
    n = jnp.where(n >= length // 2, n - length, n)
    n = jnp.where(line >= count, length // 2, n)
    ny = n.astype(jnp.float32)
    odd_y = jnp.where(n == length // 2, 0.0, ny)
    single = packed | (line >= count)
    unit = 2.0 * math.pi / length
    weight = jnp.where(single, 1.0, 2.0) * (-2.0 / (unit * float(length) * float(length) * float(layers)))
    zero = jnp.zeros((extra, rows), jnp.float32)
    items = []
    for s in range(sky):
        re = jnp.concatenate([modes[s, g, 0] for g in range(groups)], axis=0)
        im = jnp.concatenate([modes[s, g, 1] for g in range(groups)], axis=0)
        spare = jnp.broadcast_to(im[0:1], (extra, rows))
        re = jnp.concatenate([re, spare], axis=0)
        im = jnp.concatenate([im, zero], axis=0)
        items.append((re, jnp.where(packed, 0.0, im)))
    items = fft_list(items, -1.0)
    turned = []
    for k, (re, im) in enumerate(items):
        c, s = twist[k, 0:1, :], twist[k, 1:2, :]
        turned.append(jnp.concatenate([re * c + im * s, im * c - re * s], axis=1))
    spectrum = dot(jnp.concatenate(turned, axis=0), forward[...], ((1,), (0,)))
    fields = ([], [])
    for k in range(sky):
        here = spectrum[k * total : (k + 1) * total]
        re, im = here[:, :rows], here[:, rows:]
        nx = k + sky * lane
        nx = jnp.where(nx >= length // 2, nx - length, nx)
        odd_x = jnp.where(nx == -(length // 2), 0, nx).astype(jnp.float32)
        square = nx.astype(jnp.float32) * nx.astype(jnp.float32) + ny * ny
        factor = jnp.where(square == 0.0, 0.0, weight / jnp.where(square == 0.0, 1.0, square))
        for field, odd in ((0, odd_x), (1, odd_y)):
            scale = odd * factor
            fields[field].append(jnp.concatenate([-scale * im, scale * re], axis=1))
    for field in range(2):
        values = dot(jnp.concatenate(fields[field], axis=0), forward[...], ((1,), (1,)))
        items = []
        for k in range(sky):
            here = values[k * total : (k + 1) * total]
            re, im = here[:, :rows], here[:, rows:]
            c, s = twist[k, 0:1, :], twist[k, 1:2, :]
            items.append((re * c - im * s, im * c + re * s))
        items = fft_list(items, 1.0)
        for s in range(sky):
            re, im = items[s]
            im = jnp.where(packed, jnp.broadcast_to(re[count : count + 1], (total, rows)), im)
            for g in range(groups):
                outs[field][s, g, 0] = re[g * part : (g + 1) * part]
                outs[field][s, g, 1] = im[g * part : (g + 1) * part]


def plane_kernel(place, modes, table, mix, out):
    sky, groups, pair, part, rows = modes.shape
    parts, _, width = out.shape
    tiles = parts * width // LANES
    pieces = []
    for g in range(groups):
        z = jnp.concatenate([modes[d, g, j] for j in range(pair) for d in range(sky)], axis=0)
        both = dot(z, table[place[0] * groups + g], ((0,), (0,)))
        pieces.append((both[:, :LANES], both[:, LANES:]))
    for s in range(tiles):
        total = None
        for g in range(groups):
            kind = place[0] * groups + g
            term = mix[kind, 2 * s] * pieces[g][0] + mix[kind, 2 * s + 1] * pieces[g][1]
            total = term if total is None else total + term
        at = s * LANES
        relative = lax.rem(at // width - place[0] + parts, parts)
        out[relative, :, at % width : at % width + LANES] = total


def call(kernel, shapes, specs, scratch=(), work=1, grid=()):
    return pl.pallas_call(
        kernel,
        grid=grid,
        out_shape=jax.tree.map(
            lambda shape: jax.ShapeDtypeStruct(shape, jnp.float32), shapes, is_leaf=lambda s: isinstance(s[0], int)
        ),
        in_specs=specs,
        out_specs=jax.tree.map(lambda shape: VMEM, shapes, is_leaf=lambda s: isinstance(s[0], int)),
        scratch_shapes=list(scratch),
        cost_estimate=pl.CostEstimate(flops=work, bytes_accessed=work, transcendentals=0),
        compiler_params=pltpu.CompilerParams(vmem_limit_bytes=60 * 1024 * 1024),
    )


def body(density, refine, weight_low, weight_high):
    los_count = lax.axis_size("los")
    sky_count = lax.axis_size("sky")
    los = lax.axis_index("los")
    sky = lax.axis_index("sky")
    layers, rows, width = density.shape
    length = rows * sky_count
    tiles = width // LANES
    classes = tiles // 2
    groups = classes // los_count
    part = LANES // sky_count
    place = jnp.stack([los, sky]).astype(jnp.int32)
    onward = [(i, i + 1) for i in range(los_count - 1)]
    back = [(i + 1, i) for i in range(los_count - 1)]
    ring = [(i, (i + 1) % sky_count) for i in range(sky_count)]
    gnir = [((i + 1) % sky_count, i) for i in range(sky_count)]

    def to_shift(values, shift):
        return lax.ppermute(values, "los", [(i, (i + shift) % los_count) for i in range(los_count)])

    below = lax.ppermute(density[layers - 1], "los", onward)
    above = lax.ppermute(density[0], "los", back)
    first, second = density[:, 0, :], density[:, 1, :]
    former, final = density[:, rows - 2, :], density[:, rows - 1, :]
    before = lax.ppermute(final, "sky", ring)
    after = lax.ppermute(first, "sky", gnir)
    average = 0.5 * (weight_low + weight_high)
    slope = 0.125 * (weight_high - weight_low)
    keep = jnp.stack([los > 0, los < los_count - 1]).astype(jnp.float32)
    sums = call(
        sums_kernel,
        (4, rows, width),
        [VMEM, SMEM, SMEM],
        [pltpu.VMEM((layers, rows + 2 * SUB, width), jnp.float32)],
        work=40_000_000,
    )(density, average, slope)
    two = (2, rows, width)
    folded, rims = call(
        edge_kernel,
        ((los_count, groups, 2, rows, LANES), (2, classes, 2, LANES)),
        [
            VMEM,
            pl.BlockSpec(two, lambda i: (0, 0, 0), memory_space=pltpu.VMEM),
            pl.BlockSpec(two, lambda i: (layers // 2 - 1, 0, 0), memory_space=pltpu.VMEM),
        ]
        + [VMEM] * 10
        + [SMEM] * 3,
        [
            pltpu.VMEM((rows + 2 * SUB, width), jnp.float32),
            pltpu.VMEM((rows + 4 * SUB, width), jnp.float32),
            pltpu.VMEM((rows + 4 * SUB, width), jnp.float32),
        ],
        grid=(1,),
    )(
        sums, density, density, below, above, before, first, second, former, final, after, refine[0],
        average[:, None], slope, keep, place,
    )
    others = [to_shift(folded[shift], shift) for shift in range(1, los_count)]
    from_before = lax.ppermute(rims[1], "sky", ring)
    from_after = lax.ppermute(rims[0], "sky", gnir)
    rims = jnp.stack([from_before, from_after])

    def rims_of(shift):
        return lax.dynamic_slice_in_dim(rims, (los + shift) % los_count * groups, groups, 1)

    gathered = rims_of(0)
    for shift in range(1, los_count):
        gathered = gathered + to_shift(rims_of(shift), shift)
    table = row_table(width)
    block = (sky_count, groups, 2, part, rows)
    modes = call(row_kernel, block, [SMEM] + [VMEM] * (los_count + 2))(place, folded[0], *others, gathered, table)
    modes = lax.all_to_all(modes, "sky", split_axis=0, concat_axis=0, tiled=True)
    forward, twist = column_tables(length, sky_count)
    fields = call(
        functools.partial(column_kernel, length, layers * los_count),
        (block, block),
        [SMEM, VMEM, VMEM, VMEM],
    )(place, modes, forward, twist)
    mix = tile_table(width)
    results = []
    for field in fields:
        if results:
            field, results[0] = lax.optimization_barrier((field, results[0]))
        field = lax.all_to_all(field, "sky", split_axis=0, concat_axis=0, tiled=True)
        results.append(
            call(plane_kernel, (los_count, rows, width // los_count), [SMEM, VMEM, VMEM, SMEM])(
                place, field, table, mix
            )
        )
    planes = []
    for result in results:
        plane = result[0]
        for shift in range(1, los_count):
            plane = plane + to_shift(result[shift], shift)
        planes.append(plane)
    return tuple(planes)


def solution(mesh):
    placed = (P("los", "sky", None), P("los", "sky", None), P("los"), P("los"))
    return jax.shard_map(
        body,
        mesh=mesh,
        in_specs=placed,
        out_specs=(P("sky", "los"), P("sky", "los")),
        check_vma=False,
    )
```

```python
import functools
import math

import jax
import jax.numpy as jnp
import numpy as np
from jax import lax
from jax.experimental import pallas as pl
from jax.experimental.pallas import tpu as pltpu
from jax.sharding import PartitionSpec as P

LANES = 128
SUB = 8
VMEM = pl.BlockSpec(memory_space=pltpu.VMEM)
SMEM = pl.BlockSpec(memory_space=pltpu.SMEM)


def median0(a, b):
    return jnp.maximum(jnp.minimum(a, b), jnp.minimum(jnp.maximum(a, b), 0.0))


def add(p, q):
    im = q[1] if p[1] is None else (p[1] if q[1] is None else p[1] + q[1])
    return (p[0] + q[0], im)


def sub(p, q):
    if q[1] is None:
        return (p[0] - q[0], p[1])
    return (p[0] - q[0], -q[1] if p[1] is None else p[1] - q[1])


def turn(p, angle):
    c, s = math.cos(angle), math.sin(angle)
    re, im = p
    if abs(s) < 1e-12:
        return p if c > 0 else (-re, None if im is None else -im)
    if abs(c) < 1e-12:
        sign = 1.0 if s > 0 else -1.0
        if im is None:
            return (jnp.zeros_like(re), sign * re)
        return (-im, re) if s > 0 else (im, -re)
    if im is None:
        return (c * re, s * re)
    return (c * re - s * im, s * re + c * im)


def fft_list(items, flip):
    count = len(items)
    if count == 1:
        return items
    even = fft_list(items[0::2], flip)
    odd = fft_list(items[1::2], flip)
    first, second = [], []
    for k in range(count // 2):
        w = turn(odd[k], flip * 2.0 * math.pi * k / count)
        first.append(add(even[k], w))
        second.append(sub(even[k], w))
    return first + second


def row_table(width):
    tiles = width // LANES
    classes = tiles // 2
    half = LANES // 2
    t = np.arange(LANES)
    table = np.zeros((classes, 2 * LANES, 2 * LANES))

    def angles(n):
        return 2.0 * np.pi * ((n[:, None] * t[None, :]) % width) / width

    for c in range(classes):
        if c == 0:
            j = np.arange(half)
            low = angles(tiles * j)
            high = angles(tiles * j + classes)
            table[0, :half, :LANES] = np.cos(low)
            table[0, half:LANES, LANES:] = np.cos(high)
            table[0, LANES : LANES + half, :LANES] = -np.sin(low)
            table[0, LANES, :LANES] = np.cos(np.pi * t)
            table[0, LANES + half :, LANES:] = -np.sin(high)
        else:
            a = angles(c + tiles * np.arange(LANES))
            table[c, :LANES, :LANES] = np.cos(a)
            table[c, :LANES, LANES:] = np.sin(a)
            table[c, LANES:, :LANES] = -np.sin(a)
            table[c, LANES:, LANES:] = np.cos(a)
    return jnp.asarray(table, jnp.float32)


def tile_table(width):
    tiles = width // LANES
    classes = tiles // 2
    s = np.arange(tiles)
    table = np.zeros((classes, 2 * tiles))
    for c in range(classes):
        if c == 0:
            table[c, 0::2] = 1.0
            table[c, 1::2] = np.where(s % 2 == 0, 1.0, -1.0)
        else:
            table[c, 0::2] = np.cos(2.0 * np.pi * s * c / tiles)
            table[c, 1::2] = -np.sin(2.0 * np.pi * s * c / tiles)
    return jnp.asarray(table, jnp.float32)


def column_tables(length, sky):
    rows = length // sky
    t = np.arange(rows)
    a = 2.0 * np.pi * (t[:, None] * t[None, :] % rows) / rows
    c, s = np.cos(a), np.sin(a)
    forward = np.block([[c, -s], [s, c]])
    b = 2.0 * np.pi * (np.arange(sky)[:, None] * t[None, :]) / length
    twist = np.stack([np.cos(b), np.sin(b)], axis=1)
    return jnp.asarray(forward, jnp.float32), jnp.asarray(twist, jnp.float32)


def dot(a, b, dims):
    return lax.dot_general(
        a, b, (dims, ((), ())), precision=lax.Precision.HIGHEST, preferred_element_type=jnp.float32
    )


def sums_kernel(density, average, slope, out, cells):
    layers, rows, width = density.shape
    deep = 16
    last = density[:, rows - deep : rows, :]
    head = density[:, 0:deep, :]
    for z in range(layers):
        cells[z, SUB - 1 : SUB, :] = head[z].astype(jnp.float32)[0:1]
        cells[z, SUB + rows : SUB + rows + 1, :] = last[z].astype(jnp.float32)[deep - 1 : deep]

    def fill(r, carry):
        start = pl.multiple_of(r * deep, deep)
        into = pl.ds(pl.multiple_of(start + SUB, SUB), deep)
        for z in range(layers):
            cells[z, into, :] = density[z, pl.ds(start, deep), :].astype(jnp.float32)
        return carry

    lax.fori_loop(0, rows // deep, fill, 0)

    def chunk(r, carry):
        start = pl.multiple_of(r * SUB, SUB)
        here = pl.ds(pl.multiple_of(start + SUB, SUB), SUB)
        mid = cells[0, here, :]
        step_z = None
        base = jnp.zeros((SUB, width), jnp.float32)
        tilt_z, tilt_x, tilt_y = base, base, base
        for z in range(layers):
            w = cells[z, pl.ds(start, 3 * SUB), :]
            up, down = w[SUB - 1 : 2 * SUB - 1], w[SUB + 1 : 2 * SUB + 1]
            step_y = pltpu.roll(mid, width - 1, 1) - mid
            back_y = pltpu.roll(step_y, 1, 1)
            base = base + average[z] * mid
            tilt_x = tilt_x + average[z] * median0(down - mid, mid - up)
            tilt_y = tilt_y + average[z] * median0(step_y, back_y)
            if z < layers - 1:
                above = cells[z + 1, here, :]
                next_z = above - mid
                if z > 0:
                    tilt_z = tilt_z + slope[z] * median0(next_z, step_z)
                mid, step_z = above, next_z
        rows_at = pl.ds(start, SUB)
        out[0, rows_at, :] = base
        out[1, rows_at, :] = tilt_z
        out[2, rows_at, :] = tilt_x
        out[3, rows_at, :] = tilt_y
        return carry

    lax.fori_loop(0, rows // SUB, chunk, 0)


def edge_kernel(
    sums, low, high, below, above, before, first, second, former, final, after, refine, column_average, slope, keep,
    place, out, rims, base_s, smooth_s, tilt_s
):
    rows, width = below.shape
    tiles = width // LANES
    los_count, groups = out.shape[0], out.shape[1]
    blocks, coarse = refine.shape
    deep = 16
    weight = column_average[...]

    def rim_slope(one, two, three):
        one, two, three = [ref[...].astype(jnp.float32) for ref in (one, two, three)]
        return jnp.sum(weight * median0(three - two, two - one), axis=0, keepdims=True)

    fix_first = rim_slope(before, first, second)
    fix_last = rim_slope(former, final, after)
    blank = jnp.zeros((2 * SUB, width), jnp.float32)
    for ref in (smooth_s, tilt_s):
        ref[0 : 2 * SUB, :] = blank
        ref[rows + 2 * SUB : rows + 4 * SUB, :] = blank
    base_s[0:SUB, :] = blank[:SUB]
    base_s[rows + SUB : rows + 2 * SUB, :] = blank[:SUB]
    column = lax.broadcasted_iota(jnp.int32, (coarse, width), 1)
    line = lax.broadcasted_iota(jnp.int32, (coarse, width), 0)
    wide = width // coarse
    inside = (column >= line * wide) & (column < line * wide + wide)
    stretch = jnp.where(inside, 1.0, 0.0).astype(jnp.bfloat16)
    marks = jnp.dot(
        refine[...].astype(jnp.float32).astype(jnp.bfloat16), stretch, preferred_element_type=jnp.float32
    )
    for r in range(blocks):
        base_s[SUB * (r + 1) : SUB * (r + 2), :] = jnp.broadcast_to(marks[r : r + 1], (SUB, width))

    def spread(field):
        return 0.75 * field + 0.125 * (pltpu.roll(field, 1, 1) + pltpu.roll(field, width - 1, 1))

    end = low.shape[0]

    def chunk(r, carry):
        start = pl.multiple_of(r * deep, deep)
        here = pl.ds(start, deep)
        base, tilt_z, tilt_x, tilt_y = [sums[i, here, :] for i in range(4)]
        v0, v1 = [low[i, here, :].astype(jnp.float32) for i in range(2)]
        v6, v7 = [high[i, here, :].astype(jnp.float32) for i in range(2)]
        under, over = below[here, :].astype(jnp.float32), above[here, :].astype(jnp.float32)
        tilt_z = tilt_z + slope[0] * median0(v1 - v0, keep[0] * (v0 - under))
        tilt_z = tilt_z + slope[slope.shape[0] - 1] * median0(keep[1] * (over - v7), v7 - v6)
        at = lax.broadcasted_iota(jnp.int32, (deep, width), 0) + start
        tilt_x = tilt_x + jnp.where(at == 0, fix_first, 0.0) + jnp.where(at == rows - 1, fix_last, 0.0)
        ours = pl.ds(pl.multiple_of(start + SUB, SUB), deep)
        mark = base_s[ours, :]
        refined = mark * base
        base_s[ours, :] = base - refined
        tilt_y = mark * tilt_y
        into = pl.ds(pl.multiple_of(start + 2 * SUB, SUB), deep)
        smooth_s[into, :] = spread(refined + mark * tilt_z) + (
            pltpu.roll(tilt_y, 1, 1) - pltpu.roll(tilt_y, width - 1, 1)
        ) * (1.0 / 32.0)
        tilt_s[into, :] = spread(mark * tilt_x)
        return carry

    lax.fori_loop(0, rows // deep, chunk, 0)

    def pairs(start):
        a = smooth_s[pl.ds(start, 3 * SUB), :]
        b = tilt_s[pl.ds(start, 3 * SUB), :]
        prior, mid, later = slice(SUB - 1, 2 * SUB - 1), slice(SUB, 2 * SUB), slice(SUB + 1, 2 * SUB + 1)
        deposit = (
            base_s[pl.ds(start, SUB), :]
            + 0.75 * a[mid]
            + 0.125 * (a[prior] + a[later])
            + (b[prior] - b[later]) * (1.0 / 32.0)
        )
        parts = [(deposit[:, LANES * s : LANES * (s + 1)], None) for s in range(tiles)]
        modes = fft_list(parts, -1.0)
        return [(modes[0][0], modes[tiles // 2][0])] + modes[1 : tiles // 2]

    def finish(r, carry):
        into = pl.ds(pl.multiple_of(r * SUB, SUB), SUB)
        for c, pair in enumerate(pairs(pl.multiple_of((r + 1) * SUB, SUB))):
            relative = lax.rem(c // groups - place[0] + los_count, los_count)
            for j in range(2):
                out[relative, c % groups, j, into, :] = pair[j]
        return carry

    lax.fori_loop(0, rows // SUB, finish, 0)
    for edge, (start, row) in enumerate(((0, SUB - 1), (rows + SUB, 0))):
        for c, pair in enumerate(pairs(start)):
            for j in range(2):
                rims[edge, c, j : j + 1, :] = pair[j][row : row + 1]


def reach(values):
    return jnp.max(values, axis=1, keepdims=True), jnp.min(values, axis=1, keepdims=True)


def encode(first, second):
    top, low = zip(reach(first), reach(second))
    span = jnp.maximum(top[0] - low[0], top[1] - low[1])
    size = jnp.maximum(
        jnp.maximum(jnp.abs(top[0]), jnp.abs(low[0])), jnp.maximum(jnp.abs(top[1]), jnp.abs(low[1]))
    )
    span = jnp.maximum(jnp.maximum(span, size * (1.0 / 64.0)), 1e-25)
    power = jnp.ceil(jnp.log2(span * (1.0 / 65000.0)))
    inverse = jnp.exp2(-power)
    codes, offsets = [], []
    for values, t, l in ((first, top[0], low[0]), (second, top[1], low[1])):
        offset = jnp.floor(0.5 * (t + l) * inverse + 0.5)
        codes.append(jnp.floor(values * inverse - offset + 0.5).astype(jnp.int32))
        offsets.append(offset)
    return lax.shift_left(codes[0], jnp.full_like(codes[0], 16)) + (codes[1] & 65535), [power] + offsets


def decode(words, notes):
    power, one, two = notes
    step = jnp.exp2(power)
    shift = jnp.full_like(words, 16)
    first = lax.shift_right_arithmetic(words, shift).astype(jnp.float32)
    second = lax.shift_right_arithmetic(lax.shift_left(words, shift), shift).astype(jnp.float32)
    return (first + one) * step, (second + two) * step


def note_masks(count, lanes, shift):
    line = lax.broadcasted_iota(jnp.int32, (count, lanes), 0)
    lane = lax.broadcasted_iota(jnp.int32, (count, lanes), 1)
    return lane == line + shift


def pack_notes(notes, lanes):
    count = notes[0].shape[0]
    total = None
    for i, note in enumerate(notes):
        term = jnp.where(note_masks(count, lanes, i * count), note, 0.0)
        total = term if total is None else total + term
    row = jnp.sum(total, axis=0, keepdims=True)
    return jnp.broadcast_to(row, (SUB, lanes)).astype(jnp.int32)


def unpack_notes(row, count, number):
    lanes = row.shape[1]
    row = row.astype(jnp.float32)
    return [
        jnp.sum(jnp.where(note_masks(count, lanes, i * count), row, 0.0), axis=1, keepdims=True)
        for i in range(number)
    ]


def put(out, d, re, im):
    count, lanes = re.shape
    words, notes = encode(re, im)
    out[d, :count] = words
    out[d, count:] = pack_notes(notes, lanes)


def take(ref, d):
    count = ref.shape[1] - SUB
    return decode(ref[d, :count], unpack_notes(ref[d, count:][0:1], count, 3))


def row_kernel(place, own, *refs):
    *others, rims, table, out = refs
    groups, pair, rows, lanes = own.shape
    sky = out.shape[0]
    part = lanes // sky
    line = lax.broadcasted_iota(jnp.int32, (rows, lanes), 0)
    spectra = []
    for g in range(groups):
        sides = []
        for j in range(pair):
            side = own[g, j]
            for other in others:
                side = side + other[g, j]
            side = side + jnp.where(line == 0, rims[0, g, j : j + 1, :], 0.0)
            side = side + jnp.where(line == rows - 1, rims[1, g, j : j + 1, :], 0.0)
            sides.append(side)
        spectra.append(dot(table[place[0] * groups + g], jnp.concatenate(sides, axis=1), ((1,), (1,))))
    for d in range(sky):
        re, im = [
            jnp.concatenate([z[j * lanes + d * part : j * lanes + (d + 1) * part] for z in spectra], axis=0)
            for j in range(pair)
        ]
        put(out, d, re, im)


def column_kernel(length, layers, groups, place, modes, forward, twist, *outs):
    sky, _, rows = modes.shape
    part = LANES // sky
    classes = length // LANES // 2
    tiles = 2 * classes
    count = groups * part
    extra = SUB
    total = count + extra
    line = lax.broadcasted_iota(jnp.int32, (total, rows), 0)
    lane = lax.broadcasted_iota(jnp.int32, (total, rows), 1)
    first = (place[0] == 0) & (place[1] == 0)
    packed = (line == 0) & first
    group = line // part
    kind = place[0] * groups + group
    j = place[1] * part + line % part
    half = LANES // 2
    n = jnp.where(kind == 0, jnp.where(j < half, tiles * j, tiles * (j - half) + classes), kind + tiles * j)
    n = jnp.where(n >= length // 2, n - length, n)
    n = jnp.where(line >= count, length // 2, n)
    ny = n.astype(jnp.float32)
    odd_y = jnp.where(n == length // 2, 0.0, ny)
    single = packed | (line >= count)
    unit = 2.0 * math.pi / length
    weight = jnp.where(single, 1.0, 2.0) * (-2.0 / (unit * float(length) * float(length) * float(layers)))
    zero = jnp.zeros((extra, rows), jnp.float32)
    items = []
    for s in range(sky):
        re, im = take(modes, s)
        spare = jnp.broadcast_to(im[0:1], (extra, rows))
        re = jnp.concatenate([re, spare], axis=0)
        im = jnp.concatenate([im, zero], axis=0)
        items.append((re, jnp.where(packed, 0.0, im)))
    items = fft_list(items, -1.0)
    turned = []
    for k, (re, im) in enumerate(items):
        c, s = twist[k, 0:1, :], twist[k, 1:2, :]
        turned.append(jnp.concatenate([re * c + im * s, im * c - re * s], axis=1))
    spectrum = dot(jnp.concatenate(turned, axis=0), forward[...], ((1,), (0,)))
    fields = ([], [])
    for k in range(sky):
        here = spectrum[k * total : (k + 1) * total]
        re, im = here[:, :rows], here[:, rows:]
        nx = k + sky * lane
        nx = jnp.where(nx >= length // 2, nx - length, nx)
        odd_x = jnp.where(nx == -(length // 2), 0, nx).astype(jnp.float32)
        square = nx.astype(jnp.float32) * nx.astype(jnp.float32) + ny * ny
        factor = jnp.where(square == 0.0, 0.0, weight / jnp.where(square == 0.0, 1.0, square))
        for field, odd in ((0, odd_x), (1, odd_y)):
            scale = odd * factor
            fields[field].append(jnp.concatenate([-scale * im, scale * re], axis=1))
    for field in range(2):
        values = dot(jnp.concatenate(fields[field], axis=0), forward[...], ((1,), (1,)))
        items = []
        for k in range(sky):
            here = values[k * total : (k + 1) * total]
            re, im = here[:, :rows], here[:, rows:]
            c, s = twist[k, 0:1, :], twist[k, 1:2, :]
            items.append((re * c - im * s, im * c + re * s))
        items = fft_list(items, 1.0)
        for s in range(sky):
            re, im = items[s]
            im = jnp.where(packed, jnp.broadcast_to(re[count : count + 1], (total, rows)), im)
            put(outs[field], s, re[:count], im[:count])


def plane_kernel(groups, place, modes, table, mix, own, *outs):
    sky, _, rows = modes.shape
    part = LANES // sky
    width = own.shape[1]
    parts = len(outs) + 1
    inner = width // LANES
    halves = inner // 2
    blocks = [take(modes, d) for d in range(sky)]
    pieces = []
    for g in range(groups):
        z = jnp.concatenate([block[j][g * part : (g + 1) * part] for j in range(2) for block in blocks], axis=0)
        both = dot(z, table[place[0] * groups + g], ((0,), (0,)))
        pieces.append((both[:, :LANES], both[:, LANES:]))
    for relative in range(parts):
        owner = lax.rem(place[0] + relative, parts)
        sums = []
        for i in range(inner):
            total = None
            for g in range(groups):
                kind = place[0] * groups + g
                at = 2 * (owner * inner + i)
                term = mix[kind, at] * pieces[g][0] + mix[kind, at + 1] * pieces[g][1]
                total = term if total is None else total + term
            sums.append(total)
        if relative == 0:
            for i in range(inner):
                own[:, i * LANES : (i + 1) * LANES] = sums[i]
        else:
            out = outs[relative - 1]
            words, notes = encode(
                jnp.concatenate(sums[:halves], axis=1), jnp.concatenate(sums[halves:], axis=1)
            )
            out[:rows] = words
            for i, note in enumerate(notes):
                out[rows + i * SUB : rows + (i + 1) * SUB, :LANES] = pack_notes([note], LANES)
                for tile in range(1, halves):
                    out[rows + i * SUB : rows + (i + 1) * SUB, tile * LANES : (tile + 1) * LANES] = jnp.zeros(
                        (SUB, LANES), jnp.int32
                    )


def join_kernel(own, *refs):
    *others, out = refs
    rows, width = own.shape
    totals = [own[:, : width // 2], own[:, width // 2 :]]
    for other in others:
        notes = [unpack_notes(other[rows + i * SUB : rows + i * SUB + 1, :LANES], rows, 1)[0] for i in range(3)]
        for half, values in enumerate(decode(other[:rows], notes)):
            totals[half] = totals[half] + values
    out[:, : width // 2] = totals[0]
    out[:, width // 2 :] = totals[1]


def call(kernel, shapes, specs, scratch=(), work=1, grid=(), types=jnp.float32):
    if not isinstance(types, tuple):
        types = jax.tree.map(lambda shape: types, shapes, is_leaf=lambda s: isinstance(s[0], int))
    return pl.pallas_call(
        kernel,
        grid=grid,
        out_shape=jax.tree.map(
            jax.ShapeDtypeStruct, shapes, types, is_leaf=lambda s: isinstance(s[0], int)
        ),
        in_specs=specs,
        out_specs=jax.tree.map(lambda shape: VMEM, shapes, is_leaf=lambda s: isinstance(s[0], int)),
        scratch_shapes=list(scratch),
        cost_estimate=pl.CostEstimate(flops=work, bytes_accessed=work, transcendentals=0),
        compiler_params=pltpu.CompilerParams(vmem_limit_bytes=60 * 1024 * 1024),
    )


def body(density, refine, weight_low, weight_high):
    los_count = lax.axis_size("los")
    sky_count = lax.axis_size("sky")
    los = lax.axis_index("los")
    sky = lax.axis_index("sky")
    layers, rows, width = density.shape
    length = rows * sky_count
    tiles = width // LANES
    classes = tiles // 2
    groups = classes // los_count
    part = LANES // sky_count
    place = jnp.stack([los, sky]).astype(jnp.int32)
    onward = [(i, i + 1) for i in range(los_count - 1)]
    back = [(i + 1, i) for i in range(los_count - 1)]
    ring = [(i, (i + 1) % sky_count) for i in range(sky_count)]
    gnir = [((i + 1) % sky_count, i) for i in range(sky_count)]

    def to_shift(values, shift):
        return lax.ppermute(values, "los", [(i, (i + shift) % los_count) for i in range(los_count)])

    below = lax.ppermute(density[layers - 1], "los", onward)
    above = lax.ppermute(density[0], "los", back)
    first, second = density[:, 0, :], density[:, 1, :]
    former, final = density[:, rows - 2, :], density[:, rows - 1, :]
    before = lax.ppermute(final, "sky", ring)
    after = lax.ppermute(first, "sky", gnir)
    average = 0.5 * (weight_low + weight_high)
    slope = 0.125 * (weight_high - weight_low)
    keep = jnp.stack([los > 0, los < los_count - 1]).astype(jnp.float32)
    sums = call(
        sums_kernel,
        (4, rows, width),
        [VMEM, SMEM, SMEM],
        [pltpu.VMEM((layers, rows + 2 * SUB, width), jnp.float32)],
        work=40_000_000,
    )(density, average, slope)
    two = (2, rows, width)
    folded, rims = call(
        edge_kernel,
        ((los_count, groups, 2, rows, LANES), (2, classes, 2, LANES)),
        [
            VMEM,
            pl.BlockSpec(two, lambda i: (0, 0, 0), memory_space=pltpu.VMEM),
            pl.BlockSpec(two, lambda i: (layers // 2 - 1, 0, 0), memory_space=pltpu.VMEM),
        ]
        + [VMEM] * 10
        + [SMEM] * 3,
        [
            pltpu.VMEM((rows + 2 * SUB, width), jnp.float32),
            pltpu.VMEM((rows + 4 * SUB, width), jnp.float32),
            pltpu.VMEM((rows + 4 * SUB, width), jnp.float32),
        ],
        grid=(1,),
    )(
        sums, density, density, below, above, before, first, second, former, final, after, refine[0],
        average[:, None], slope, keep, place,
    )
    others = [to_shift(folded[shift], shift) for shift in range(1, los_count)]
    from_before = lax.ppermute(rims[1], "sky", ring)
    from_after = lax.ppermute(rims[0], "sky", gnir)
    rims = jnp.stack([from_before, from_after])

    def rims_of(shift):
        return lax.dynamic_slice_in_dim(rims, (los + shift) % los_count * groups, groups, 1)

    gathered = rims_of(0)
    for shift in range(1, los_count):
        gathered = gathered + to_shift(rims_of(shift), shift)
    table = row_table(width)
    block = (sky_count, groups * part + SUB, rows)
    modes = call(row_kernel, block, [SMEM] + [VMEM] * (los_count + 2), types=jnp.int32)(
        place, folded[0], *others, gathered, table
    )
    modes = lax.all_to_all(modes, "sky", split_axis=0, concat_axis=0, tiled=True)
    forward, twist = column_tables(length, sky_count)
    fields = call(
        functools.partial(column_kernel, length, layers * los_count, groups),
        (block, block),
        [SMEM, VMEM, VMEM, VMEM],
        types=jnp.int32,
    )(place, modes, forward, twist)
    mix = tile_table(width)
    out_width = width // los_count
    shapes = ((rows, out_width),) + ((rows + 3 * SUB, out_width // 2),) * (los_count - 1)
    results = []
    for field in fields:
        if results:
            field, results[0] = lax.optimization_barrier((field, results[0]))
        field = lax.all_to_all(field, "sky", split_axis=0, concat_axis=0, tiled=True)
        results.append(
            call(
                functools.partial(plane_kernel, groups),
                shapes,
                [SMEM, VMEM, VMEM, SMEM],
                types=(jnp.float32,) + (jnp.int32,) * (los_count - 1),
            )(place, field, table, mix)
        )
    planes = []
    for own, *sent in results:
        got = [to_shift(words, shift) for shift, words in enumerate(sent, 1)]
        planes.append(call(join_kernel, (rows, out_width), [VMEM] * los_count)(own, *got))
    return tuple(planes)


def solution(mesh):
    placed = (P("los", "sky", None), P("los", "sky", None), P("los"), P("los"))
    return jax.shard_map(
        body,
        mesh=mesh,
        in_specs=placed,
        out_specs=(P("sky", "los"), P("sky", "los")),
        check_vma=False,
    )
```

```python
import functools
import math

import jax
import jax.numpy as jnp
import numpy as np
from jax import lax
from jax.experimental import pallas as pl
from jax.experimental.pallas import tpu as pltpu
from jax.sharding import PartitionSpec as P

LANES = 128
SUB = 8
VMEM = pl.BlockSpec(memory_space=pltpu.VMEM)
SMEM = pl.BlockSpec(memory_space=pltpu.SMEM)


def median0(a, b):
    return jnp.maximum(jnp.minimum(a, b), jnp.minimum(jnp.maximum(a, b), 0.0))


def add(p, q):
    im = q[1] if p[1] is None else (p[1] if q[1] is None else p[1] + q[1])
    return (p[0] + q[0], im)


def sub(p, q):
    if q[1] is None:
        return (p[0] - q[0], p[1])
    return (p[0] - q[0], -q[1] if p[1] is None else p[1] - q[1])


def turn(p, angle):
    c, s = math.cos(angle), math.sin(angle)
    re, im = p
    if abs(s) < 1e-12:
        return p if c > 0 else (-re, None if im is None else -im)
    if abs(c) < 1e-12:
        sign = 1.0 if s > 0 else -1.0
        if im is None:
            return (jnp.zeros_like(re), sign * re)
        return (-im, re) if s > 0 else (im, -re)
    if im is None:
        return (c * re, s * re)
    return (c * re - s * im, s * re + c * im)


def fft_list(items, flip):
    count = len(items)
    if count == 1:
        return items
    even = fft_list(items[0::2], flip)
    odd = fft_list(items[1::2], flip)
    first, second = [], []
    for k in range(count // 2):
        w = turn(odd[k], flip * 2.0 * math.pi * k / count)
        first.append(add(even[k], w))
        second.append(sub(even[k], w))
    return first + second


def row_table(width):
    tiles = width // LANES
    classes = tiles // 2
    half = LANES // 2
    t = np.arange(LANES)
    table = np.zeros((classes, 2 * LANES, 2 * LANES))

    def angles(n):
        return 2.0 * np.pi * ((n[:, None] * t[None, :]) % width) / width

    for c in range(classes):
        if c == 0:
            j = np.arange(half)
            low = angles(tiles * j)
            high = angles(tiles * j + classes)
            table[0, :half, :LANES] = np.cos(low)
            table[0, half:LANES, LANES:] = np.cos(high)
            table[0, LANES : LANES + half, :LANES] = -np.sin(low)
            table[0, LANES, :LANES] = np.cos(np.pi * t)
            table[0, LANES + half :, LANES:] = -np.sin(high)
        else:
            a = angles(c + tiles * np.arange(LANES))
            table[c, :LANES, :LANES] = np.cos(a)
            table[c, :LANES, LANES:] = np.sin(a)
            table[c, LANES:, :LANES] = -np.sin(a)
            table[c, LANES:, LANES:] = np.cos(a)
    return jnp.asarray(table, jnp.float32)


def tile_table(width):
    tiles = width // LANES
    classes = tiles // 2
    s = np.arange(tiles)
    table = np.zeros((classes, 2 * tiles))
    for c in range(classes):
        if c == 0:
            table[c, 0::2] = 1.0
            table[c, 1::2] = np.where(s % 2 == 0, 1.0, -1.0)
        else:
            table[c, 0::2] = np.cos(2.0 * np.pi * s * c / tiles)
            table[c, 1::2] = -np.sin(2.0 * np.pi * s * c / tiles)
    return jnp.asarray(table, jnp.float32)


def column_tables(length, sky):
    rows = length // sky
    t = np.arange(rows)
    a = 2.0 * np.pi * (t[:, None] * t[None, :] % rows) / rows
    c, s = np.cos(a), np.sin(a)
    forward = np.block([[c, -s], [s, c]])
    b = 2.0 * np.pi * (np.arange(sky)[:, None] * t[None, :]) / length
    twist = np.stack([np.cos(b), np.sin(b)], axis=1)
    return jnp.asarray(forward, jnp.float32), jnp.asarray(twist, jnp.float32)


def dot(a, b, dims):
    return lax.dot_general(
        a, b, (dims, ((), ())), precision=lax.Precision.HIGHEST, preferred_element_type=jnp.float32
    )


def sums_kernel(density, average, slope, out, cells):
    layers, rows, width = density.shape
    deep = 16
    last = density[:, rows - deep : rows, :]
    head = density[:, 0:deep, :]
    for z in range(layers):
        cells[z, SUB - 1 : SUB, :] = head[z].astype(jnp.float32)[0:1]
        cells[z, SUB + rows : SUB + rows + 1, :] = last[z].astype(jnp.float32)[deep - 1 : deep]

    def fill(r, carry):
        start = pl.multiple_of(r * deep, deep)
        into = pl.ds(pl.multiple_of(start + SUB, SUB), deep)
        for z in range(layers):
            cells[z, into, :] = density[z, pl.ds(start, deep), :].astype(jnp.float32)
        return carry

    lax.fori_loop(0, rows // deep, fill, 0)

    def chunk(r, carry):
        start = pl.multiple_of(r * SUB, SUB)
        here = pl.ds(pl.multiple_of(start + SUB, SUB), SUB)
        mid = cells[0, here, :]
        step_z = None
        base = jnp.zeros((SUB, width), jnp.float32)
        tilt_z, tilt_x, tilt_y = base, base, base
        for z in range(layers):
            w = cells[z, pl.ds(start, 3 * SUB), :]
            up, down = w[SUB - 1 : 2 * SUB - 1], w[SUB + 1 : 2 * SUB + 1]
            step_y = pltpu.roll(mid, width - 1, 1) - mid
            back_y = pltpu.roll(step_y, 1, 1)
            base = base + average[z] * mid
            tilt_x = tilt_x + average[z] * median0(down - mid, mid - up)
            tilt_y = tilt_y + average[z] * median0(step_y, back_y)
            if z < layers - 1:
                above = cells[z + 1, here, :]
                next_z = above - mid
                if z > 0:
                    tilt_z = tilt_z + slope[z] * median0(next_z, step_z)
                mid, step_z = above, next_z
        rows_at = pl.ds(start, SUB)
        out[0, rows_at, :] = base
        out[1, rows_at, :] = tilt_z
        out[2, rows_at, :] = tilt_x
        out[3, rows_at, :] = tilt_y
        return carry

    lax.fori_loop(0, rows // SUB, chunk, 0)


def edge_kernel(
    sums, low, high, below, above, before, first, second, former, final, after, refine, column_average, slope, keep,
    place, out, rims, base_s, smooth_s, tilt_s
):
    rows, width = below.shape
    tiles = width // LANES
    los_count, groups = out.shape[0], out.shape[1]
    blocks, coarse = refine.shape
    deep = 16
    weight = column_average[...]

    def rim_slope(one, two, three):
        one, two, three = [ref[...].astype(jnp.float32) for ref in (one, two, three)]
        return jnp.sum(weight * median0(three - two, two - one), axis=0, keepdims=True)

    fix_first = rim_slope(before, first, second)
    fix_last = rim_slope(former, final, after)
    blank = jnp.zeros((2 * SUB, width), jnp.float32)
    for ref in (smooth_s, tilt_s):
        ref[0 : 2 * SUB, :] = blank
        ref[rows + 2 * SUB : rows + 4 * SUB, :] = blank
    base_s[0:SUB, :] = blank[:SUB]
    base_s[rows + SUB : rows + 2 * SUB, :] = blank[:SUB]
    column = lax.broadcasted_iota(jnp.int32, (coarse, width), 1)
    line = lax.broadcasted_iota(jnp.int32, (coarse, width), 0)
    wide = width // coarse
    inside = (column >= line * wide) & (column < line * wide + wide)
    stretch = jnp.where(inside, 1.0, 0.0).astype(jnp.bfloat16)
    marks = jnp.dot(
        refine[...].astype(jnp.float32).astype(jnp.bfloat16), stretch, preferred_element_type=jnp.float32
    )
    for r in range(blocks):
        base_s[SUB * (r + 1) : SUB * (r + 2), :] = jnp.broadcast_to(marks[r : r + 1], (SUB, width))

    def spread(field):
        return 0.75 * field + 0.125 * (pltpu.roll(field, 1, 1) + pltpu.roll(field, width - 1, 1))

    end = low.shape[0]

    def chunk(r, carry):
        start = pl.multiple_of(r * deep, deep)
        here = pl.ds(start, deep)
        base, tilt_z, tilt_x, tilt_y = [sums[i, here, :] for i in range(4)]
        v0, v1 = [low[i, here, :].astype(jnp.float32) for i in range(2)]
        v6, v7 = [high[i, here, :].astype(jnp.float32) for i in range(2)]
        under, over = below[here, :].astype(jnp.float32), above[here, :].astype(jnp.float32)
        tilt_z = tilt_z + slope[0] * median0(v1 - v0, keep[0] * (v0 - under))
        tilt_z = tilt_z + slope[slope.shape[0] - 1] * median0(keep[1] * (over - v7), v7 - v6)
        at = lax.broadcasted_iota(jnp.int32, (deep, width), 0) + start
        tilt_x = tilt_x + jnp.where(at == 0, fix_first, 0.0) + jnp.where(at == rows - 1, fix_last, 0.0)
        ours = pl.ds(pl.multiple_of(start + SUB, SUB), deep)
        mark = base_s[ours, :]
        refined = mark * base
        base_s[ours, :] = base - refined
        tilt_y = mark * tilt_y
        into = pl.ds(pl.multiple_of(start + 2 * SUB, SUB), deep)
        smooth_s[into, :] = spread(refined + mark * tilt_z) + (
            pltpu.roll(tilt_y, 1, 1) - pltpu.roll(tilt_y, width - 1, 1)
        ) * (1.0 / 32.0)
        tilt_s[into, :] = spread(mark * tilt_x)
        return carry

    lax.fori_loop(0, rows // deep, chunk, 0)

    def pairs(start):
        a = smooth_s[pl.ds(start, 3 * SUB), :]
        b = tilt_s[pl.ds(start, 3 * SUB), :]
        prior, mid, later = slice(SUB - 1, 2 * SUB - 1), slice(SUB, 2 * SUB), slice(SUB + 1, 2 * SUB + 1)
        deposit = (
            base_s[pl.ds(start, SUB), :]
            + 0.75 * a[mid]
            + 0.125 * (a[prior] + a[later])
            + (b[prior] - b[later]) * (1.0 / 32.0)
        )
        parts = [(deposit[:, LANES * s : LANES * (s + 1)], None) for s in range(tiles)]
        modes = fft_list(parts, -1.0)
        return [(modes[0][0], modes[tiles // 2][0])] + modes[1 : tiles // 2]

    def finish(r, carry):
        into = pl.ds(pl.multiple_of(r * SUB, SUB), SUB)
        for c, pair in enumerate(pairs(pl.multiple_of((r + 1) * SUB, SUB))):
            relative = lax.rem(c // groups - place[0] + los_count, los_count)
            for j in range(2):
                out[relative, c % groups, j, into, :] = pair[j]
        return carry

    lax.fori_loop(0, rows // SUB, finish, 0)
    for edge, (start, row) in enumerate(((0, SUB - 1), (rows + SUB, 0))):
        for c, pair in enumerate(pairs(start)):
            for j in range(2):
                rims[edge, c, j : j + 1, :] = pair[j][row : row + 1]


def reach(values):
    return jnp.max(values, axis=1, keepdims=True), jnp.min(values, axis=1, keepdims=True)


def encode(first, second):
    top, low = zip(reach(first), reach(second))
    span = jnp.maximum(top[0] - low[0], top[1] - low[1])
    size = jnp.maximum(
        jnp.maximum(jnp.abs(top[0]), jnp.abs(low[0])), jnp.maximum(jnp.abs(top[1]), jnp.abs(low[1]))
    )
    span = jnp.maximum(jnp.maximum(span, size * (1.0 / 64.0)), 1e-25)
    power = jnp.ceil(jnp.log2(span * (1.0 / 65000.0)))
    inverse = jnp.exp2(-power)
    codes, offsets = [], []
    for values, t, l in ((first, top[0], low[0]), (second, top[1], low[1])):
        offset = jnp.floor(0.5 * (t + l) * inverse + 0.5)
        codes.append(jnp.floor(values * inverse - offset + 0.5).astype(jnp.int32))
        offsets.append(offset)
    return lax.shift_left(codes[0], jnp.full_like(codes[0], 16)) + (codes[1] & 65535), [power] + offsets


def decode(words, notes):
    power, one, two = notes
    step = jnp.exp2(power)
    shift = jnp.full_like(words, 16)
    first = lax.shift_right_arithmetic(words, shift).astype(jnp.float32)
    second = lax.shift_right_arithmetic(lax.shift_left(words, shift), shift).astype(jnp.float32)
    return (first + one) * step, (second + two) * step


def note_masks(count, lanes, shift):
    line = lax.broadcasted_iota(jnp.int32, (count, lanes), 0)
    lane = lax.broadcasted_iota(jnp.int32, (count, lanes), 1)
    return lane == line + shift


def pack_notes(notes, lanes):
    count = notes[0].shape[0]
    total = None
    for i, note in enumerate(notes):
        term = jnp.where(note_masks(count, lanes, i * count), note, 0.0)
        total = term if total is None else total + term
    row = jnp.sum(total, axis=0, keepdims=True)
    return jnp.broadcast_to(row, (SUB, lanes)).astype(jnp.int32)


def unpack_notes(row, count, number):
    lanes = row.shape[1]
    row = row.astype(jnp.float32)
    return [
        jnp.sum(jnp.where(note_masks(count, lanes, i * count), row, 0.0), axis=1, keepdims=True)
        for i in range(number)
    ]


def put(out, d, re, im):
    count, lanes = re.shape
    words, notes = encode(re, im)
    out[d, :count] = words
    out[d, count:] = pack_notes(notes, lanes)


def take(ref, d):
    count = ref.shape[1] - SUB
    return decode(ref[d, :count], unpack_notes(ref[d, count:][0:1], count, 3))


def row_kernel(place, own, *refs):
    *others, rims, table, out = refs
    groups, pair, rows, lanes = own.shape
    sky = out.shape[0]
    part = lanes // sky
    line = lax.broadcasted_iota(jnp.int32, (rows, lanes), 0)
    spectra = []
    for g in range(groups):
        sides = []
        for j in range(pair):
            side = own[g, j]
            for other in others:
                side = side + other[g, j]
            side = side + jnp.where(line == 0, rims[0, g, j : j + 1, :], 0.0)
            side = side + jnp.where(line == rows - 1, rims[1, g, j : j + 1, :], 0.0)
            sides.append(side)
        spectra.append(dot(table[place[0] * groups + g], jnp.concatenate(sides, axis=1), ((1,), (1,))))
    for d in range(sky):
        re, im = [
            jnp.concatenate([z[j * lanes + d * part : j * lanes + (d + 1) * part] for z in spectra], axis=0)
            for j in range(pair)
        ]
        put(out, d, re, im)


def column_kernel(length, layers, groups, place, modes, forward, twist, *outs):
    sky, _, rows = modes.shape
    part = LANES // sky
    classes = length // LANES // 2
    tiles = 2 * classes
    count = groups * part
    extra = SUB
    total = count + extra
    line = lax.broadcasted_iota(jnp.int32, (total, rows), 0)
    lane = lax.broadcasted_iota(jnp.int32, (total, rows), 1)
    first = (place[0] == 0) & (place[1] == 0)
    packed = (line == 0) & first
    group = line // part
    kind = place[0] * groups + group
    j = place[1] * part + line % part
    half = LANES // 2
    n = jnp.where(kind == 0, jnp.where(j < half, tiles * j, tiles * (j - half) + classes), kind + tiles * j)
    n = jnp.where(n >= length // 2, n - length, n)
    n = jnp.where(line >= count, length // 2, n)
    ny = n.astype(jnp.float32)
    odd_y = jnp.where(n == length // 2, 0.0, ny)
    single = packed | (line >= count)
    unit = 2.0 * math.pi / length
    weight = jnp.where(single, 1.0, 2.0) * (-2.0 / (unit * float(length) * float(length) * float(layers)))
    zero = jnp.zeros((extra, rows), jnp.float32)
    items = []
    for s in range(sky):
        re, im = take(modes, s)
        spare = jnp.broadcast_to(im[0:1], (extra, rows))
        re = jnp.concatenate([re, spare], axis=0)
        im = jnp.concatenate([im, zero], axis=0)
        items.append((re, jnp.where(packed, 0.0, im)))
    items = fft_list(items, -1.0)
    turned = []
    for k, (re, im) in enumerate(items):
        c, s = twist[k, 0:1, :], twist[k, 1:2, :]
        turned.append(jnp.concatenate([re * c + im * s, im * c - re * s], axis=1))
    spectrum = dot(jnp.concatenate(turned, axis=0), forward[...], ((1,), (0,)))
    fields = ([], [])
    for k in range(sky):
        here = spectrum[k * total : (k + 1) * total]
        re, im = here[:, :rows], here[:, rows:]
        nx = k + sky * lane
        nx = jnp.where(nx >= length // 2, nx - length, nx)
        odd_x = jnp.where(nx == -(length // 2), 0, nx).astype(jnp.float32)
        square = nx.astype(jnp.float32) * nx.astype(jnp.float32) + ny * ny
        factor = jnp.where(square == 0.0, 0.0, weight / jnp.where(square == 0.0, 1.0, square))
        for field, odd in ((0, odd_x), (1, odd_y)):
            scale = odd * factor
            fields[field].append(jnp.concatenate([-scale * im, scale * re], axis=1))
    for field in range(2):
        values = dot(jnp.concatenate(fields[field], axis=0), forward[...], ((1,), (1,)))
        items = []
        for k in range(sky):
            here = values[k * total : (k + 1) * total]
            re, im = here[:, :rows], here[:, rows:]
            c, s = twist[k, 0:1, :], twist[k, 1:2, :]
            items.append((re * c - im * s, im * c + re * s))
        items = fft_list(items, 1.0)
        for s in range(sky):
            re, im = items[s]
            im = jnp.where(packed, jnp.broadcast_to(re[count : count + 1], (total, rows)), im)
            put(outs[field], s, re[:count], im[:count])


def plane_kernel(groups, place, modes, table, mix, own, *outs):
    sky, _, rows = modes.shape
    part = LANES // sky
    width = own.shape[1]
    parts = len(outs) + 1
    inner = width // LANES
    halves = inner // 2
    blocks = [take(modes, d) for d in range(sky)]
    pieces = []
    for g in range(groups):
        z = jnp.concatenate([block[j][g * part : (g + 1) * part] for j in range(2) for block in blocks], axis=0)
        both = dot(z, table[place[0] * groups + g], ((0,), (0,)))
        pieces.append((both[:, :LANES], both[:, LANES:]))
    for relative in range(parts):
        owner = lax.rem(place[0] + relative, parts)
        sums = []
        for i in range(inner):
            total = None
            for g in range(groups):
                kind = place[0] * groups + g
                at = 2 * (owner * inner + i)
                term = mix[kind, at] * pieces[g][0] + mix[kind, at + 1] * pieces[g][1]
                total = term if total is None else total + term
            sums.append(total)
        if relative == 0:
            for i in range(inner):
                own[:, i * LANES : (i + 1) * LANES] = sums[i]
        else:
            out = outs[relative - 1]
            words, notes = encode(
                jnp.concatenate(sums[:halves], axis=1), jnp.concatenate(sums[halves:], axis=1)
            )
            out[:rows] = words
            for i, note in enumerate(notes):
                out[rows + i * SUB : rows + (i + 1) * SUB, :LANES] = pack_notes([note], LANES)
                for tile in range(1, halves):
                    out[rows + i * SUB : rows + (i + 1) * SUB, tile * LANES : (tile + 1) * LANES] = jnp.zeros(
                        (SUB, LANES), jnp.int32
                    )


def exchange_kernel(source, target, send, receive, local):
    me = lax.axis_index("sky")
    count = source.shape[0]
    barrier = pltpu.get_barrier_semaphore()
    for i in range(1, count):
        pl.semaphore_signal(
            barrier, inc=1, device_id={"sky": lax.rem(me + i, count)}, device_id_type=pl.DeviceIdType.MESH
        )
    own = pltpu.make_async_copy(source.at[me], target.at[me], local)
    own.start()
    pl.semaphore_wait(barrier, count - 1)
    copies = []
    for i in range(1, count):
        peer = lax.rem(me + i, count)
        copies.append(
            pltpu.make_async_remote_copy(
                src_ref=source.at[peer],
                dst_ref=target.at[me],
                send_sem=send.at[i],
                recv_sem=receive.at[i],
                device_id={"sky": peer},
                device_id_type=pl.DeviceIdType.MESH,
            )
        )
        copies[-1].start()
    own.wait()
    for copy in copies:
        copy.wait()


def exchange(values, number):
    count = values.shape[0]
    return pl.pallas_call(
        exchange_kernel,
        out_shape=jax.ShapeDtypeStruct(values.shape, values.dtype),
        in_specs=[VMEM],
        out_specs=VMEM,
        scratch_shapes=[
            pltpu.SemaphoreType.DMA((count,)),
            pltpu.SemaphoreType.DMA((count,)),
            pltpu.SemaphoreType.DMA,
        ],
        compiler_params=pltpu.CompilerParams(collective_id=number, has_side_effects=True),
    )(values)


def join_kernel(own, *refs):
    *others, out = refs
    rows, width = own.shape
    totals = [own[:, : width // 2], own[:, width // 2 :]]
    for other in others:
        notes = [unpack_notes(other[rows + i * SUB : rows + i * SUB + 1, :LANES], rows, 1)[0] for i in range(3)]
        for half, values in enumerate(decode(other[:rows], notes)):
            totals[half] = totals[half] + values
    out[:, : width // 2] = totals[0]
    out[:, width // 2 :] = totals[1]


def call(kernel, shapes, specs, scratch=(), work=1, grid=(), types=jnp.float32):
    if not isinstance(types, tuple):
        types = jax.tree.map(lambda shape: types, shapes, is_leaf=lambda s: isinstance(s[0], int))
    return pl.pallas_call(
        kernel,
        grid=grid,
        out_shape=jax.tree.map(
            jax.ShapeDtypeStruct, shapes, types, is_leaf=lambda s: isinstance(s[0], int)
        ),
        in_specs=specs,
        out_specs=jax.tree.map(lambda shape: VMEM, shapes, is_leaf=lambda s: isinstance(s[0], int)),
        scratch_shapes=list(scratch),
        cost_estimate=pl.CostEstimate(flops=work, bytes_accessed=work, transcendentals=0),
        compiler_params=pltpu.CompilerParams(vmem_limit_bytes=60 * 1024 * 1024),
    )


def body(density, refine, weight_low, weight_high):
    los_count = lax.axis_size("los")
    sky_count = lax.axis_size("sky")
    los = lax.axis_index("los")
    sky = lax.axis_index("sky")
    layers, rows, width = density.shape
    length = rows * sky_count
    tiles = width // LANES
    classes = tiles // 2
    groups = classes // los_count
    part = LANES // sky_count
    place = jnp.stack([los, sky]).astype(jnp.int32)
    onward = [(i, i + 1) for i in range(los_count - 1)]
    back = [(i + 1, i) for i in range(los_count - 1)]
    ring = [(i, (i + 1) % sky_count) for i in range(sky_count)]
    gnir = [((i + 1) % sky_count, i) for i in range(sky_count)]

    def to_shift(values, shift):
        return lax.ppermute(values, "los", [(i, (i + shift) % los_count) for i in range(los_count)])

    below = lax.ppermute(density[layers - 1], "los", onward)
    above = lax.ppermute(density[0], "los", back)
    first, second = density[:, 0, :], density[:, 1, :]
    former, final = density[:, rows - 2, :], density[:, rows - 1, :]
    before = lax.ppermute(final, "sky", ring)
    after = lax.ppermute(first, "sky", gnir)
    average = 0.5 * (weight_low + weight_high)
    slope = 0.125 * (weight_high - weight_low)
    keep = jnp.stack([los > 0, los < los_count - 1]).astype(jnp.float32)
    sums = call(
        sums_kernel,
        (4, rows, width),
        [VMEM, SMEM, SMEM],
        [pltpu.VMEM((layers, rows + 2 * SUB, width), jnp.float32)],
        work=40_000_000,
    )(density, average, slope)
    two = (2, rows, width)
    folded, rims = call(
        edge_kernel,
        ((los_count, groups, 2, rows, LANES), (2, classes, 2, LANES)),
        [
            VMEM,
            pl.BlockSpec(two, lambda i: (0, 0, 0), memory_space=pltpu.VMEM),
            pl.BlockSpec(two, lambda i: (layers // 2 - 1, 0, 0), memory_space=pltpu.VMEM),
        ]
        + [VMEM] * 10
        + [SMEM] * 3,
        [
            pltpu.VMEM((rows + 2 * SUB, width), jnp.float32),
            pltpu.VMEM((rows + 4 * SUB, width), jnp.float32),
            pltpu.VMEM((rows + 4 * SUB, width), jnp.float32),
        ],
        grid=(1,),
    )(
        sums, density, density, below, above, before, first, second, former, final, after, refine[0],
        average[:, None], slope, keep, place,
    )
    others = [to_shift(folded[shift], shift) for shift in range(1, los_count)]
    from_before = lax.ppermute(rims[1], "sky", ring)
    from_after = lax.ppermute(rims[0], "sky", gnir)
    rims = jnp.stack([from_before, from_after])

    def rims_of(shift):
        return lax.dynamic_slice_in_dim(rims, (los + shift) % los_count * groups, groups, 1)

    gathered = rims_of(0)
    for shift in range(1, los_count):
        gathered = gathered + to_shift(rims_of(shift), shift)
    table = row_table(width)
    block = (sky_count, groups * part + SUB, rows)
    modes = call(row_kernel, block, [SMEM] + [VMEM] * (los_count + 2), types=jnp.int32)(
        place, folded[0], *others, gathered, table
    )
    modes = exchange(modes, 0)
    forward, twist = column_tables(length, sky_count)
    fields = call(
        functools.partial(column_kernel, length, layers * los_count, groups),
        (block, block),
        [SMEM, VMEM, VMEM, VMEM],
        types=jnp.int32,
    )(place, modes, forward, twist)
    mix = tile_table(width)
    out_width = width // los_count
    shapes = ((rows, out_width),) + ((rows + 3 * SUB, out_width // 2),) * (los_count - 1)
    results = []
    for number, field in enumerate(fields, 1):
        if results:
            field, results[0] = lax.optimization_barrier((field, results[0]))
        field = exchange(field, number)
        results.append(
            call(
                functools.partial(plane_kernel, groups),
                shapes,
                [SMEM, VMEM, VMEM, SMEM],
                types=(jnp.float32,) + (jnp.int32,) * (los_count - 1),
            )(place, field, table, mix)
        )
    planes = []
    for own, *sent in results:
        got = [to_shift(words, shift) for shift, words in enumerate(sent, 1)]
        planes.append(call(join_kernel, (rows, out_width), [VMEM] * los_count)(own, *got))
    return tuple(planes)


def solution(mesh):
    placed = (P("los", "sky", None), P("los", "sky", None), P("los"), P("los"))
    return jax.shard_map(
        body,
        mesh=mesh,
        in_specs=placed,
        out_specs=(P("sky", "los"), P("sky", "los")),
        check_vma=False,
    )
```

```python
import functools
import math

import jax
import jax.numpy as jnp
import numpy as np
from jax import lax
from jax.experimental import pallas as pl
from jax.experimental.pallas import tpu as pltpu
from jax.sharding import PartitionSpec as P

LANES = 128
SUB = 8
VMEM = pl.BlockSpec(memory_space=pltpu.VMEM)
SMEM = pl.BlockSpec(memory_space=pltpu.SMEM)


def median0(a, b):
    return jnp.maximum(jnp.minimum(a, b), jnp.minimum(jnp.maximum(a, b), 0.0))


def add(p, q):
    im = q[1] if p[1] is None else (p[1] if q[1] is None else p[1] + q[1])
    return (p[0] + q[0], im)


def sub(p, q):
    if q[1] is None:
        return (p[0] - q[0], p[1])
    return (p[0] - q[0], -q[1] if p[1] is None else p[1] - q[1])


def turn(p, angle):
    c, s = math.cos(angle), math.sin(angle)
    re, im = p
    if abs(s) < 1e-12:
        return p if c > 0 else (-re, None if im is None else -im)
    if abs(c) < 1e-12:
        sign = 1.0 if s > 0 else -1.0
        if im is None:
            return (jnp.zeros_like(re), sign * re)
        return (-im, re) if s > 0 else (im, -re)
    if im is None:
        return (c * re, s * re)
    return (c * re - s * im, s * re + c * im)


def fft_list(items, flip):
    count = len(items)
    if count == 1:
        return items
    even = fft_list(items[0::2], flip)
    odd = fft_list(items[1::2], flip)
    first, second = [], []
    for k in range(count // 2):
        w = turn(odd[k], flip * 2.0 * math.pi * k / count)
        first.append(add(even[k], w))
        second.append(sub(even[k], w))
    return first + second


def row_table(width):
    tiles = width // LANES
    classes = tiles // 2
    half = LANES // 2
    t = np.arange(LANES)
    table = np.zeros((classes, 2 * LANES, 2 * LANES))

    def angles(n):
        return 2.0 * np.pi * ((n[:, None] * t[None, :]) % width) / width

    for c in range(classes):
        if c == 0:
            j = np.arange(half)
            low = angles(tiles * j)
            high = angles(tiles * j + classes)
            table[0, :half, :LANES] = np.cos(low)
            table[0, half:LANES, LANES:] = np.cos(high)
            table[0, LANES : LANES + half, :LANES] = -np.sin(low)
            table[0, LANES, :LANES] = np.cos(np.pi * t)
            table[0, LANES + half :, LANES:] = -np.sin(high)
        else:
            a = angles(c + tiles * np.arange(LANES))
            table[c, :LANES, :LANES] = np.cos(a)
            table[c, :LANES, LANES:] = np.sin(a)
            table[c, LANES:, :LANES] = -np.sin(a)
            table[c, LANES:, LANES:] = np.cos(a)
    return jnp.asarray(table, jnp.float32)


def tile_table(width):
    tiles = width // LANES
    classes = tiles // 2
    s = np.arange(tiles)
    table = np.zeros((classes, 2 * tiles))
    for c in range(classes):
        if c == 0:
            table[c, 0::2] = 1.0
            table[c, 1::2] = np.where(s % 2 == 0, 1.0, -1.0)
        else:
            table[c, 0::2] = np.cos(2.0 * np.pi * s * c / tiles)
            table[c, 1::2] = -np.sin(2.0 * np.pi * s * c / tiles)
    return jnp.asarray(table, jnp.float32)


def column_tables(length, sky):
    rows = length // sky
    t = np.arange(rows)
    a = 2.0 * np.pi * (t[:, None] * t[None, :] % rows) / rows
    c, s = np.cos(a), np.sin(a)
    forward = np.block([[c, -s], [s, c]])
    b = 2.0 * np.pi * (np.arange(sky)[:, None] * t[None, :]) / length
    twist = np.stack([np.cos(b), np.sin(b)], axis=1)
    return jnp.asarray(forward, jnp.float32), jnp.asarray(twist, jnp.float32)


def dot(a, b, dims):
    return lax.dot_general(
        a, b, (dims, ((), ())), precision=lax.Precision.HIGHEST, preferred_element_type=jnp.float32
    )


def sums_kernel(
    average, slope, density, first, final, out, below, above, before, after, cells, send, receive
):
    layers, rows, width = density.shape
    los, sky = lax.axis_index("los"), lax.axis_index("sky")
    los_count, sky_count = lax.axis_size("los"), lax.axis_size("sky")
    barrier = pltpu.get_barrier_semaphore()
    mesh = pl.DeviceIdType.MESH
    for axis, me, count in (("los", los, los_count), ("sky", sky, sky_count)):
        for shift in (1, count - 1):
            pl.semaphore_signal(barrier, inc=1, device_id={axis: lax.rem(me + shift, count)}, device_id_type=mesh)
    pl.semaphore_wait(barrier, 4)

    def hop(source, target, i, axis, me, count, shift):
        return pltpu.make_async_remote_copy(
            src_ref=source,
            dst_ref=target,
            send_sem=send.at[i],
            recv_sem=receive.at[i],
            device_id={axis: lax.rem(me + shift, count)},
            device_id_type=mesh,
        )

    onward = hop(density.at[layers - 1], below, 0, "los", los, los_count, 1)
    back = hop(density.at[0], above, 1, "los", los, los_count, los_count - 1)
    forth = hop(final, before, 2, "sky", sky, sky_count, 1)
    prior = hop(first, after, 3, "sky", sky, sky_count, sky_count - 1)
    has_next, has_prior = los < los_count - 1, los > 0
    pl.when(has_next)(onward.start)
    pl.when(has_prior)(back.start)
    forth.start()
    prior.start()
    deep = 16
    last = density[:, rows - deep : rows, :]
    head = density[:, 0:deep, :]
    for z in range(layers):
        cells[z, SUB - 1 : SUB, :] = head[z].astype(jnp.float32)[0:1]
        cells[z, SUB + rows : SUB + rows + 1, :] = last[z].astype(jnp.float32)[deep - 1 : deep]

    def fill(r, carry):
        start = pl.multiple_of(r * deep, deep)
        into = pl.ds(pl.multiple_of(start + SUB, SUB), deep)
        for z in range(layers):
            cells[z, into, :] = density[z, pl.ds(start, deep), :].astype(jnp.float32)
        return carry

    lax.fori_loop(0, rows // deep, fill, 0)

    def chunk(r, carry):
        start = pl.multiple_of(r * SUB, SUB)
        here = pl.ds(pl.multiple_of(start + SUB, SUB), SUB)
        mid = cells[0, here, :]
        step_z = None
        base = jnp.zeros((SUB, width), jnp.float32)
        tilt_z, tilt_x, tilt_y = base, base, base
        for z in range(layers):
            w = cells[z, pl.ds(start, 3 * SUB), :]
            up, down = w[SUB - 1 : 2 * SUB - 1], w[SUB + 1 : 2 * SUB + 1]
            step_y = pltpu.roll(mid, width - 1, 1) - mid
            back_y = pltpu.roll(step_y, 1, 1)
            base = base + average[z] * mid
            tilt_x = tilt_x + average[z] * median0(down - mid, mid - up)
            tilt_y = tilt_y + average[z] * median0(step_y, back_y)
            if z < layers - 1:
                above = cells[z + 1, here, :]
                next_z = above - mid
                if z > 0:
                    tilt_z = tilt_z + slope[z] * median0(next_z, step_z)
                mid, step_z = above, next_z
        rows_at = pl.ds(start, SUB)
        out[0, rows_at, :] = base
        out[1, rows_at, :] = tilt_z
        out[2, rows_at, :] = tilt_x
        out[3, rows_at, :] = tilt_y
        return carry

    lax.fori_loop(0, rows // SUB, chunk, 0)
    forth.wait()
    prior.wait()
    pl.when(has_next)(onward.wait_send)
    pl.when(has_prior)(onward.wait_recv)
    pl.when(has_prior)(back.wait_send)
    pl.when(has_next)(back.wait_recv)


def edge_kernel(
    sums, low, high, below, above, before, first, second, former, final, after, refine, column_average, slope, keep,
    place, out, rims, base_s, smooth_s, tilt_s
):
    rows, width = below.shape
    tiles = width // LANES
    los_count, groups = out.shape[0], out.shape[1]
    blocks, coarse = refine.shape
    deep = 16
    weight = column_average[...]

    def rim_slope(one, two, three):
        one, two, three = [ref[...].astype(jnp.float32) for ref in (one, two, three)]
        return jnp.sum(weight * median0(three - two, two - one), axis=0, keepdims=True)

    fix_first = rim_slope(before, first, second)
    fix_last = rim_slope(former, final, after)
    blank = jnp.zeros((2 * SUB, width), jnp.float32)
    for ref in (smooth_s, tilt_s):
        ref[0 : 2 * SUB, :] = blank
        ref[rows + 2 * SUB : rows + 4 * SUB, :] = blank
    base_s[0:SUB, :] = blank[:SUB]
    base_s[rows + SUB : rows + 2 * SUB, :] = blank[:SUB]
    column = lax.broadcasted_iota(jnp.int32, (coarse, width), 1)
    line = lax.broadcasted_iota(jnp.int32, (coarse, width), 0)
    wide = width // coarse
    inside = (column >= line * wide) & (column < line * wide + wide)
    stretch = jnp.where(inside, 1.0, 0.0).astype(jnp.bfloat16)
    marks = jnp.dot(
        refine[...].astype(jnp.float32).astype(jnp.bfloat16), stretch, preferred_element_type=jnp.float32
    )
    for r in range(blocks):
        base_s[SUB * (r + 1) : SUB * (r + 2), :] = jnp.broadcast_to(marks[r : r + 1], (SUB, width))

    def spread(field):
        return 0.75 * field + 0.125 * (pltpu.roll(field, 1, 1) + pltpu.roll(field, width - 1, 1))

    end = low.shape[0]

    def chunk(r, carry):
        start = pl.multiple_of(r * deep, deep)
        here = pl.ds(start, deep)
        base, tilt_z, tilt_x, tilt_y = [sums[i, here, :] for i in range(4)]
        v0, v1 = [low[i, here, :].astype(jnp.float32) for i in range(2)]
        v6, v7 = [high[i, here, :].astype(jnp.float32) for i in range(2)]
        under, over = below[here, :].astype(jnp.float32), above[here, :].astype(jnp.float32)
        tilt_z = tilt_z + slope[0] * median0(v1 - v0, jnp.where(keep[0] > 0.0, v0 - under, 0.0))
        tilt_z = tilt_z + slope[slope.shape[0] - 1] * median0(jnp.where(keep[1] > 0.0, over - v7, 0.0), v7 - v6)
        at = lax.broadcasted_iota(jnp.int32, (deep, width), 0) + start
        tilt_x = tilt_x + jnp.where(at == 0, fix_first, 0.0) + jnp.where(at == rows - 1, fix_last, 0.0)
        ours = pl.ds(pl.multiple_of(start + SUB, SUB), deep)
        mark = base_s[ours, :]
        refined = mark * base
        base_s[ours, :] = base - refined
        tilt_y = mark * tilt_y
        into = pl.ds(pl.multiple_of(start + 2 * SUB, SUB), deep)
        smooth_s[into, :] = spread(refined + mark * tilt_z) + (
            pltpu.roll(tilt_y, 1, 1) - pltpu.roll(tilt_y, width - 1, 1)
        ) * (1.0 / 32.0)
        tilt_s[into, :] = spread(mark * tilt_x)
        return carry

    lax.fori_loop(0, rows // deep, chunk, 0)

    def pairs(start):
        a = smooth_s[pl.ds(start, 3 * SUB), :]
        b = tilt_s[pl.ds(start, 3 * SUB), :]
        prior, mid, later = slice(SUB - 1, 2 * SUB - 1), slice(SUB, 2 * SUB), slice(SUB + 1, 2 * SUB + 1)
        deposit = (
            base_s[pl.ds(start, SUB), :]
            + 0.75 * a[mid]
            + 0.125 * (a[prior] + a[later])
            + (b[prior] - b[later]) * (1.0 / 32.0)
        )
        parts = [(deposit[:, LANES * s : LANES * (s + 1)], None) for s in range(tiles)]
        modes = fft_list(parts, -1.0)
        return [(modes[0][0], modes[tiles // 2][0])] + modes[1 : tiles // 2]

    def finish(r, carry):
        into = pl.ds(pl.multiple_of(r * SUB, SUB), SUB)
        for c, pair in enumerate(pairs(pl.multiple_of((r + 1) * SUB, SUB))):
            relative = lax.rem(c // groups - place[0] + los_count, los_count)
            for j in range(2):
                out[relative, c % groups, j, into, :] = pair[j]
        return carry

    lax.fori_loop(0, rows // SUB, finish, 0)
    for edge, (start, row) in enumerate(((0, SUB - 1), (rows + SUB, 0))):
        for c, pair in enumerate(pairs(start)):
            for j in range(2):
                rims[edge, c, j : j + 1, :] = pair[j][row : row + 1]


def reach(values):
    return jnp.max(values, axis=1, keepdims=True), jnp.min(values, axis=1, keepdims=True)


def encode(first, second):
    top, low = zip(reach(first), reach(second))
    span = jnp.maximum(top[0] - low[0], top[1] - low[1])
    size = jnp.maximum(
        jnp.maximum(jnp.abs(top[0]), jnp.abs(low[0])), jnp.maximum(jnp.abs(top[1]), jnp.abs(low[1]))
    )
    span = jnp.maximum(jnp.maximum(span, size * (1.0 / 64.0)), 1e-25)
    power = jnp.ceil(jnp.log2(span * (1.0 / 65000.0)))
    inverse = jnp.exp2(-power)
    codes, offsets = [], []
    for values, t, l in ((first, top[0], low[0]), (second, top[1], low[1])):
        offset = jnp.floor(0.5 * (t + l) * inverse + 0.5)
        codes.append(jnp.floor(values * inverse - offset + 0.5).astype(jnp.int32))
        offsets.append(offset)
    return lax.shift_left(codes[0], jnp.full_like(codes[0], 16)) + (codes[1] & 65535), [power] + offsets


def decode(words, notes):
    power, one, two = notes
    step = jnp.exp2(power)
    shift = jnp.full_like(words, 16)
    first = lax.shift_right_arithmetic(words, shift).astype(jnp.float32)
    second = lax.shift_right_arithmetic(lax.shift_left(words, shift), shift).astype(jnp.float32)
    return (first + one) * step, (second + two) * step


def note_masks(count, lanes, shift):
    line = lax.broadcasted_iota(jnp.int32, (count, lanes), 0)
    lane = lax.broadcasted_iota(jnp.int32, (count, lanes), 1)
    return lane == line + shift


def pack_notes(notes, lanes):
    count = notes[0].shape[0]
    total = None
    for i, note in enumerate(notes):
        term = jnp.where(note_masks(count, lanes, i * count), note, 0.0)
        total = term if total is None else total + term
    row = jnp.sum(total, axis=0, keepdims=True)
    return jnp.broadcast_to(row, (SUB, lanes)).astype(jnp.int32)


def unpack_notes(row, count, number):
    lanes = row.shape[1]
    row = row.astype(jnp.float32)
    return [
        jnp.sum(jnp.where(note_masks(count, lanes, i * count), row, 0.0), axis=1, keepdims=True)
        for i in range(number)
    ]


def put(out, d, re, im):
    count, lanes = re.shape
    words, notes = encode(re, im)
    out[d, :count] = words
    out[d, count:] = pack_notes(notes, lanes)


def take(ref, d):
    count = ref.shape[1] - SUB
    return decode(ref[d, :count], unpack_notes(ref[d, count:][0:1], count, 3))


def row_kernel(place, own, *refs):
    *others, rims, table, out = refs
    groups, pair, rows, lanes = own.shape
    sky = out.shape[0]
    part = lanes // sky
    line = lax.broadcasted_iota(jnp.int32, (rows, lanes), 0)
    spectra = []
    for g in range(groups):
        sides = []
        for j in range(pair):
            side = own[g, j]
            for other in others:
                side = side + other[g, j]
            side = side + jnp.where(line == 0, rims[0, g, j : j + 1, :], 0.0)
            side = side + jnp.where(line == rows - 1, rims[1, g, j : j + 1, :], 0.0)
            sides.append(side)
        spectra.append(dot(table[place[0] * groups + g], jnp.concatenate(sides, axis=1), ((1,), (1,))))
    for d in range(sky):
        re, im = [
            jnp.concatenate([z[j * lanes + d * part : j * lanes + (d + 1) * part] for z in spectra], axis=0)
            for j in range(pair)
        ]
        put(out, d, re, im)


def column_kernel(length, layers, groups, place, modes, forward, twist, *outs):
    sky, _, rows = modes.shape
    part = LANES // sky
    classes = length // LANES // 2
    tiles = 2 * classes
    count = groups * part
    extra = SUB
    total = count + extra
    line = lax.broadcasted_iota(jnp.int32, (total, rows), 0)
    lane = lax.broadcasted_iota(jnp.int32, (total, rows), 1)
    first = (place[0] == 0) & (place[1] == 0)
    packed = (line == 0) & first
    group = line // part
    kind = place[0] * groups + group
    j = place[1] * part + line % part
    half = LANES // 2
    n = jnp.where(kind == 0, jnp.where(j < half, tiles * j, tiles * (j - half) + classes), kind + tiles * j)
    n = jnp.where(n >= length // 2, n - length, n)
    n = jnp.where(line >= count, length // 2, n)
    ny = n.astype(jnp.float32)
    odd_y = jnp.where(n == length // 2, 0.0, ny)
    single = packed | (line >= count)
    unit = 2.0 * math.pi / length
    weight = jnp.where(single, 1.0, 2.0) * (-2.0 / (unit * float(length) * float(length) * float(layers)))
    zero = jnp.zeros((extra, rows), jnp.float32)
    items = []
    for s in range(sky):
        re, im = take(modes, s)
        spare = jnp.broadcast_to(im[0:1], (extra, rows))
        re = jnp.concatenate([re, spare], axis=0)
        im = jnp.concatenate([im, zero], axis=0)
        items.append((re, jnp.where(packed, 0.0, im)))
    items = fft_list(items, -1.0)
    turned = []
    for k, (re, im) in enumerate(items):
        c, s = twist[k, 0:1, :], twist[k, 1:2, :]
        turned.append(jnp.concatenate([re * c + im * s, im * c - re * s], axis=1))
    spectrum = dot(jnp.concatenate(turned, axis=0), forward[...], ((1,), (0,)))
    fields = ([], [])
    for k in range(sky):
        here = spectrum[k * total : (k + 1) * total]
        re, im = here[:, :rows], here[:, rows:]
        nx = k + sky * lane
        nx = jnp.where(nx >= length // 2, nx - length, nx)
        odd_x = jnp.where(nx == -(length // 2), 0, nx).astype(jnp.float32)
        square = nx.astype(jnp.float32) * nx.astype(jnp.float32) + ny * ny
        factor = jnp.where(square == 0.0, 0.0, weight / jnp.where(square == 0.0, 1.0, square))
        for field, odd in ((0, odd_x), (1, odd_y)):
            scale = odd * factor
            fields[field].append(jnp.concatenate([-scale * im, scale * re], axis=1))
    for field in range(2):
        values = dot(jnp.concatenate(fields[field], axis=0), forward[...], ((1,), (1,)))
        items = []
        for k in range(sky):
            here = values[k * total : (k + 1) * total]
            re, im = here[:, :rows], here[:, rows:]
            c, s = twist[k, 0:1, :], twist[k, 1:2, :]
            items.append((re * c - im * s, im * c + re * s))
        items = fft_list(items, 1.0)
        for s in range(sky):
            re, im = items[s]
            im = jnp.where(packed, jnp.broadcast_to(re[count : count + 1], (total, rows)), im)
            put(outs[field], s, re[:count], im[:count])


def plane_kernel(groups, place, modes, table, mix, own, *outs):
    sky, _, rows = modes.shape
    part = LANES // sky
    width = own.shape[1]
    parts = len(outs) + 1
    inner = width // LANES
    halves = inner // 2
    blocks = [take(modes, d) for d in range(sky)]
    pieces = []
    for g in range(groups):
        z = jnp.concatenate([block[j][g * part : (g + 1) * part] for j in range(2) for block in blocks], axis=0)
        both = dot(z, table[place[0] * groups + g], ((0,), (0,)))
        pieces.append((both[:, :LANES], both[:, LANES:]))
    for relative in range(parts):
        owner = lax.rem(place[0] + relative, parts)
        sums = []
        for i in range(inner):
            total = None
            for g in range(groups):
                kind = place[0] * groups + g
                at = 2 * (owner * inner + i)
                term = mix[kind, at] * pieces[g][0] + mix[kind, at + 1] * pieces[g][1]
                total = term if total is None else total + term
            sums.append(total)
        if relative == 0:
            for i in range(inner):
                own[:, i * LANES : (i + 1) * LANES] = sums[i]
        else:
            out = outs[relative - 1]
            words, notes = encode(
                jnp.concatenate(sums[:halves], axis=1), jnp.concatenate(sums[halves:], axis=1)
            )
            out[:rows] = words
            for i, note in enumerate(notes):
                out[rows + i * SUB : rows + (i + 1) * SUB, :LANES] = pack_notes([note], LANES)
                for tile in range(1, halves):
                    out[rows + i * SUB : rows + (i + 1) * SUB, tile * LANES : (tile + 1) * LANES] = jnp.zeros(
                        (SUB, LANES), jnp.int32
                    )


def exchange_kernel(source, target, send, receive, local):
    me = lax.axis_index("sky")
    count = source.shape[0]
    barrier = pltpu.get_barrier_semaphore()
    for i in range(1, count):
        pl.semaphore_signal(
            barrier, inc=1, device_id={"sky": lax.rem(me + i, count)}, device_id_type=pl.DeviceIdType.MESH
        )
    own = pltpu.make_async_copy(source.at[me], target.at[me], local)
    own.start()
    pl.semaphore_wait(barrier, count - 1)
    copies = []
    for i in range(1, count):
        peer = lax.rem(me + i, count)
        copies.append(
            pltpu.make_async_remote_copy(
                src_ref=source.at[peer],
                dst_ref=target.at[me],
                send_sem=send.at[i],
                recv_sem=receive.at[i],
                device_id={"sky": peer},
                device_id_type=pl.DeviceIdType.MESH,
            )
        )
        copies[-1].start()
    own.wait()
    for copy in copies:
        copy.wait()


def exchange(values, number):
    count = values.shape[0]
    return pl.pallas_call(
        exchange_kernel,
        out_shape=jax.ShapeDtypeStruct(values.shape, values.dtype),
        in_specs=[VMEM],
        out_specs=VMEM,
        scratch_shapes=[
            pltpu.SemaphoreType.DMA((count,)),
            pltpu.SemaphoreType.DMA((count,)),
            pltpu.SemaphoreType.DMA,
        ],
        compiler_params=pltpu.CompilerParams(collective_id=number, has_side_effects=True),
    )(values)


def join_kernel(own, *refs):
    *others, out = refs
    rows, width = own.shape
    totals = [own[:, : width // 2], own[:, width // 2 :]]
    for other in others:
        notes = [unpack_notes(other[rows + i * SUB : rows + i * SUB + 1, :LANES], rows, 1)[0] for i in range(3)]
        for half, values in enumerate(decode(other[:rows], notes)):
            totals[half] = totals[half] + values
    out[:, : width // 2] = totals[0]
    out[:, width // 2 :] = totals[1]


def call(kernel, shapes, specs, scratch=(), work=1, grid=(), types=jnp.float32, number=None):
    if not isinstance(types, tuple):
        types = jax.tree.map(lambda shape: types, shapes, is_leaf=lambda s: isinstance(s[0], int))
    return pl.pallas_call(
        kernel,
        grid=grid,
        out_shape=jax.tree.map(
            jax.ShapeDtypeStruct, shapes, types, is_leaf=lambda s: isinstance(s[0], int)
        ),
        in_specs=specs,
        out_specs=jax.tree.map(lambda shape: VMEM, shapes, is_leaf=lambda s: isinstance(s[0], int)),
        scratch_shapes=list(scratch),
        cost_estimate=pl.CostEstimate(flops=work, bytes_accessed=work, transcendentals=0),
        compiler_params=pltpu.CompilerParams(
            vmem_limit_bytes=60 * 1024 * 1024, collective_id=number, has_side_effects=number is not None
        ),
    )


def body(density, refine, weight_low, weight_high):
    los_count = lax.axis_size("los")
    sky_count = lax.axis_size("sky")
    los = lax.axis_index("los")
    sky = lax.axis_index("sky")
    layers, rows, width = density.shape
    length = rows * sky_count
    tiles = width // LANES
    classes = tiles // 2
    groups = classes // los_count
    part = LANES // sky_count
    place = jnp.stack([los, sky]).astype(jnp.int32)
    ring = [(i, (i + 1) % sky_count) for i in range(sky_count)]
    gnir = [((i + 1) % sky_count, i) for i in range(sky_count)]

    def to_shift(values, shift):
        return lax.ppermute(values, "los", [(i, (i + shift) % los_count) for i in range(los_count)])

    first, second = density[:, 0, :], density[:, 1, :]
    former, final = density[:, rows - 2, :], density[:, rows - 1, :]
    average = 0.5 * (weight_low + weight_high)
    slope = 0.125 * (weight_high - weight_low)
    keep = jnp.stack([los > 0, los < los_count - 1]).astype(jnp.float32)
    half = jnp.bfloat16
    sums, below, above, before, after = call(
        sums_kernel,
        ((4, rows, width), (rows, width), (rows, width), (layers, width), (layers, width)),
        [SMEM, SMEM] + [VMEM] * 3,
        [
            pltpu.VMEM((layers, rows + 2 * SUB, width), jnp.float32),
            pltpu.SemaphoreType.DMA((4,)),
            pltpu.SemaphoreType.DMA((4,)),
        ],
        work=40_000_000,
        types=(jnp.float32, half, half, half, half),
        number=3,
    )(average, slope, density, first, final)
    two = (2, rows, width)
    folded, rims = call(
        edge_kernel,
        ((los_count, groups, 2, rows, LANES), (2, classes, 2, LANES)),
        [
            VMEM,
            pl.BlockSpec(two, lambda i: (0, 0, 0), memory_space=pltpu.VMEM),
            pl.BlockSpec(two, lambda i: (layers // 2 - 1, 0, 0), memory_space=pltpu.VMEM),
        ]
        + [VMEM] * 10
        + [SMEM] * 3,
        [
            pltpu.VMEM((rows + 2 * SUB, width), jnp.float32),
            pltpu.VMEM((rows + 4 * SUB, width), jnp.float32),
            pltpu.VMEM((rows + 4 * SUB, width), jnp.float32),
        ],
        grid=(1,),
    )(
        sums, density, density, below, above, before, first, second, former, final, after, refine[0],
        average[:, None], slope, keep, place,
    )
    others = [to_shift(folded[shift], shift) for shift in range(1, los_count)]
    from_before = lax.ppermute(rims[1], "sky", ring)
    from_after = lax.ppermute(rims[0], "sky", gnir)
    rims = jnp.stack([from_before, from_after])

    def rims_of(shift):
        return lax.dynamic_slice_in_dim(rims, (los + shift) % los_count * groups, groups, 1)

    gathered = rims_of(0)
    for shift in range(1, los_count):
        gathered = gathered + to_shift(rims_of(shift), shift)
    table = row_table(width)
    block = (sky_count, groups * part + SUB, rows)
    modes = call(row_kernel, block, [SMEM] + [VMEM] * (los_count + 2), types=jnp.int32)(
        place, folded[0], *others, gathered, table
    )
    modes = exchange(modes, 0)
    forward, twist = column_tables(length, sky_count)
    fields = call(
        functools.partial(column_kernel, length, layers * los_count, groups),
        (block, block),
        [SMEM, VMEM, VMEM, VMEM],
        types=jnp.int32,
    )(place, modes, forward, twist)
    mix = tile_table(width)
    out_width = width // los_count
    shapes = ((rows, out_width),) + ((rows + 3 * SUB, out_width // 2),) * (los_count - 1)
    results = []
    for number, field in enumerate(fields, 1):
        if results:
            field, results[0] = lax.optimization_barrier((field, results[0]))
        field = exchange(field, number)
        results.append(
            call(
                functools.partial(plane_kernel, groups),
                shapes,
                [SMEM, VMEM, VMEM, SMEM],
                types=(jnp.float32,) + (jnp.int32,) * (los_count - 1),
            )(place, field, table, mix)
        )
    planes = []
    for own, *sent in results:
        got = [to_shift(words, shift) for shift, words in enumerate(sent, 1)]
        planes.append(call(join_kernel, (rows, out_width), [VMEM] * los_count)(own, *got))
    return tuple(planes)


def solution(mesh):
    placed = (P("los", "sky", None), P("los", "sky", None), P("los"), P("los"))
    return jax.shard_map(
        body,
        mesh=mesh,
        in_specs=placed,
        out_specs=(P("sky", "los"), P("sky", "los")),
        check_vma=False,
    )
```
